128 devices in a mesh: ta: 8 (over z, core), af: 16 (over x, y).
Axes of the slice: x: 4, y: 4, z: 4, core: 2. Of those that a mesh axis runs over, the one named last changes fastest.
Arguments:
- velocity: float32 [16, 512, 128, 128], P(None, ('ta', 'af')), may hold values from -14 to 14
- initial_basis: float32 [512, 64], replicated, may hold values from -6 to 6
Outputs:
- core: float32 [16, 128, 64, 128], P('ta', 'af')
The draws below stay inside these ranges and needn't reach their ends.
All inputs are finite; a program needn't handle non-finite values.
Results may differ from the reference program's by a relative error of at most 0.00017.
Values sent between devices are 32-bit elements; how exact they have to be, the bound alone decides.
A program may use at most 64 MiB of HBM per device.

```python
import math
import jax
import jax.numpy as jnp
from jax import lax

Z = 512
X = 128
Y = 128
K = 64
F = 16
ITERS = 3


def draw_velocity(key, part):
    key_scale = jax.random.fold_in(key, 11)
    key_noise = jax.random.fold_in(key, 23)
    log_scale = jax.random.uniform(key_scale, (Z,), jnp.float32, math.log(0.5), math.log(2.0))
    plane_scale = jnp.exp(log_scale)[None, :, None, None]
    fluctuation = jnp.clip(jax.random.normal(key_noise, (F, Z, X, Y), jnp.float32), -6.0, 6.0)
    return fluctuation * plane_scale


def gaussian(stream_key, extent, deviation, reach, held_as=jnp.bfloat16):
    return jnp.clip(deviation * jax.random.normal(stream_key, extent, jnp.float32), -reach, reach).astype(held_as)


def setup_inputs(seed: int = 0) -> dict:
    keys = jax.random.split(jax.random.key(seed), 3)
    velocity = draw_velocity(jax.random.fold_in(keys[2], 71), 0)
    initial_basis = gaussian(keys[1], (Z, K), 1.0, 6.0, jnp.float32)
    return dict(velocity=velocity, initial_basis=initial_basis)


def orthonormal(product):
    lower = jnp.linalg.cholesky(jnp.dot(product.T.astype(jnp.float32), product.astype(jnp.float32), precision=lax.Precision.HIGHEST, preferred_element_type=jnp.float32))
    return jax.scipy.linalg.solve_triangular(lower, product.T, lower=True).T

def reference(velocity, initial_basis):

    def accumulate(running, one_frame):
        matrix = one_frame.reshape(Z, X * Y)
        return (running + jnp.dot(matrix.astype(jnp.float32), matrix.T.astype(jnp.float32), precision=lax.Precision.HIGHEST, preferred_element_type=jnp.float32), None)
    gram_matrix, unused = lax.scan(accumulate, jnp.zeros((Z, Z), jnp.float32), velocity)
    subspace = initial_basis
    for iteration in range(ITERS):
        subspace = orthonormal(jnp.dot(gram_matrix.astype(jnp.float32), subspace.astype(jnp.float32), precision=lax.Precision.HIGHEST, preferred_element_type=jnp.float32))

    def project(one_frame):
        return jnp.einsum('zxy,zk->xky', one_frame.astype(jnp.float32), subspace.astype(jnp.float32), precision=lax.Precision.HIGHEST, preferred_element_type=jnp.float32)
    return lax.map(project, velocity)
```

```python
import functools
import itertools
import random

import jax
import jax.numpy as jnp
from jax import lax
from jax.experimental import pallas as pl
from jax.experimental.pallas import tpu as pltpu
from jax.sharding import PartitionSpec as P

ITERS = 3
MESH = pl.DeviceIdType.MESH
HIGHEST = lax.Precision.HIGHEST
F32, BF16 = jnp.float32, jnp.bfloat16
NN = (((1,), (0,)), ((), ()))
NT = (((1,), (1,)), ((), ()))


def offsets(n_ta, n_af):
    order = [o for o in itertools.product(range(n_ta), range(n_af)) if o != (0, 0)]
    random.Random(0).shuffle(order)
    return order


def split(value):
    high = value.astype(BF16)
    return high, (value - high.astype(F32)).astype(BF16)


def dot(a, b, dims):
    return lax.dot_general(a, b, dims, preferred_element_type=F32)


def wait_bytes(ref, sem):
    pltpu.make_async_copy(ref, ref, sem).wait()


def regroup_kernel(
    n_ta, n_af, velocity, gram, high_out, low_out, fibres, high, low, partial, pieces,
    send_sem, recv_sem, own_sem, out_sem, rs_send, rs_recv, ag_send, ag_recv,
):
    n = n_ta * n_af
    ta, af = lax.axis_index("ta"), lax.axis_index("af")
    me = ta * n_af + af
    frames, planes, cells = fibres.shape[0], velocity.shape[1], fibres.shape[2]
    order = offsets(n_ta, n_af)
    tas = [lax.rem(ta + i, n_ta) for i in range(n_ta)]
    afs = [lax.rem(af + i, n_af) for i in range(n_af)]

    own = []
    for f in range(frames):
        copy = pltpu.make_async_copy(
            velocity.at[frames * ta + f, :, pl.ds(cells * af, cells), :],
            fibres.at[f, pl.ds(planes * me, planes)],
            own_sem.at[f],
        )
        copy.start()
        own.append(copy)

    barrier = pltpu.get_barrier_semaphore()
    for i, j in order:
        pl.semaphore_signal(barrier, inc=1, device_id=(tas[i], afs[j]), device_id_type=MESH)
    pl.semaphore_wait(barrier, n - 1)

    for f in range(frames):
        for i, j in order:
            pltpu.make_async_remote_copy(
                src_ref=velocity.at[frames * tas[i] + f, :, pl.ds(cells * afs[j], cells), :],
                dst_ref=fibres.at[f, pl.ds(planes * me, planes)],
                send_sem=send_sem,
                recv_sem=recv_sem.at[f],
                device_id=(tas[i], afs[j]),
                device_id_type=MESH,
            ).start()

    outs = []
    for f in range(frames):
        own[f].wait()
        wait_bytes(fibres.at[f, pl.ds(0, planes * (n - 1))], recv_sem.at[f])
        for x in range(cells):
            h, l = split(fibres[f, :, x, :])
            high[f, :, 128 * x : 128 * x + 128] = h
            low[f, :, 128 * x : 128 * x + 128] = l
        for src, dst, s in ((high, high_out, 0), (low, low_out, 1)):
            copy = pltpu.make_async_copy(src.at[f], dst.at[f], out_sem.at[f, s])
            copy.start()
            outs.append(copy)
        for half in range(2):
            rows = pl.ds(256 * half, 256)
            term = (
                dot(high[f], high[f, rows, :], NT)
                + dot(low[f], high[f, rows, :], NT)
                + dot(high[f], low[f, rows, :], NT)
            )
            partial[half] = term if f == 0 else partial[half] + term
    wait_bytes(fibres.at[:, pl.ds(0, planes * (n - 1))], send_sem)

    rows = partial.shape[1] // (n // 2)
    for i, j in order:
        d = tas[i] * n_af + afs[j]
        pltpu.make_async_remote_copy(
            src_ref=partial.at[d // (n // 2), pl.ds(pl.multiple_of(rows * lax.rem(d, n // 2), rows), rows)],
            dst_ref=pieces.at[me],
            send_sem=rs_send,
            recv_sem=rs_recv,
            device_id=(tas[i], afs[j]),
            device_id_type=MESH,
        ).start()
    mine = (me // (n // 2), pl.ds(pl.multiple_of(rows * lax.rem(me, n // 2), rows), rows))
    pieces[me] = partial[mine]
    wait_bytes(pieces.at[pl.ds(0, n - 1)], rs_recv)
    gram[mine] = jnp.sum(pieces[...], axis=0)
    for i, j in order:
        pltpu.make_async_remote_copy(
            src_ref=gram.at[mine],
            dst_ref=gram.at[mine],
            send_sem=ag_send,
            recv_sem=ag_recv,
            device_id=(tas[i], afs[j]),
            device_id_type=MESH,
        ).start()
    wait_bytes(pieces.at[pl.ds(0, n - 1)], rs_send)
    wait_bytes(pieces.at[pl.ds(0, n - 1)], ag_send)
    wait_bytes(pieces.at[pl.ds(0, n - 1)], ag_recv)
    for copy in outs:
        copy.wait()


def regroup(velocity, n_ta, n_af):
    frames, planes, cells, cells_y = velocity.shape
    n = n_ta * n_af
    f, z, x = frames // n_ta, planes * n, cells // n_af
    return pl.pallas_call(
        functools.partial(regroup_kernel, n_ta, n_af),
        name="regroup",
        out_shape=(
            jax.ShapeDtypeStruct((2, z, z // 2), F32),
            jax.ShapeDtypeStruct((f, z, x * cells_y), BF16),
            jax.ShapeDtypeStruct((f, z, x * cells_y), BF16),
        ),
        in_specs=[pl.BlockSpec(memory_space=pl.ANY)],
        out_specs=(
            pl.BlockSpec(memory_space=pltpu.VMEM),
            pl.BlockSpec(memory_space=pl.ANY),
            pl.BlockSpec(memory_space=pl.ANY),
        ),
        scratch_shapes=[
            pltpu.VMEM((f, z, x, cells_y), F32),
            pltpu.VMEM((f, z, x * cells_y), BF16),
            pltpu.VMEM((f, z, x * cells_y), BF16),
            pltpu.VMEM((2, z, z // 2), F32),
            pltpu.VMEM((n, 2 * z // n, z // 2), F32),
            pltpu.SemaphoreType.DMA,
            pltpu.SemaphoreType.DMA((f,)),
            pltpu.SemaphoreType.DMA((f,)),
            pltpu.SemaphoreType.DMA((f, 2)),
            pltpu.SemaphoreType.DMA,
            pltpu.SemaphoreType.DMA,
            pltpu.SemaphoreType.DMA,
            pltpu.SemaphoreType.DMA,
        ],
        compiler_params=pltpu.CompilerParams(
            collective_id=0, has_side_effects=True, vmem_limit_bytes=48 * 2**20
        ),
    )(velocity)


def inverse_cholesky(matrix):
    k, width = matrix.shape
    groups = k // 8
    rows = [matrix[8 * r : 8 * r + 8, :] for r in range(groups)]
    sublane = lax.broadcasted_iota(jnp.int32, (8, width), 0)
    spread = lambda v, c: jnp.broadcast_to(v[c : c + 1, :], (8, width))
    pivots = []
    for g in range(groups):
        columns = [
            [jnp.broadcast_to(rows[r][:, 8 * g + c : 8 * g + c + 1], (8, width)) for r in range(g, groups)]
            for c in range(8)
        ]
        diagonal = None
        for c in range(8):
            pivot = spread(columns[c][0], c)
            diagonal = pivot if c == 0 else jnp.where(sublane == c, pivot, diagonal)
            inverse = pl.reciprocal(pivot, approx=False)
            pivot_row = spread(rows[g], c)
            pivot_columns = {d: spread(columns[d][0], c) for d in range(c + 1, 8)}
            for r in range(g, groups):
                factor = columns[c][r - g] * inverse
                if r == g:
                    factor = jnp.where(sublane > c, factor, 0.0)
                rows[r] = rows[r] - factor * pivot_row
                for d in range(c + 1, 8):
                    columns[d][r - g] = columns[d][r - g] - factor * pivot_columns[d]
        pivots.append(diagonal)
    scaled = []
    for r in range(groups):
        root = lax.rsqrt(pivots[r])
        root = root * (1.5 - 0.5 * (pivots[r] * root) * root)
        scaled.append(rows[r] * root)
    return jnp.concatenate(scaled, axis=0)


def factor_kernel(basis, gram, high_in, low_in, core, subspace, high, low, sem):
    copies = []
    for f in range(high.shape[0]):
        for s, (src, dst) in enumerate(((high_in, high), (low_in, low))):
            copy = pltpu.make_async_copy(src.at[f], dst.at[f], sem.at[f, s])
            copy.start()
            copies.append(copy)
    k, z = basis.shape
    subspace[...] = basis[...]
    row = lax.broadcasted_iota(jnp.int32, (k, 2 * k), 0)
    lane = lax.broadcasted_iota(jnp.int32, (k, 2 * k), 1)
    identity = jnp.where(lane == row + k, 1.0, 0.0).astype(F32)

    def iterate(_, carry):
        product = jnp.concatenate(
            [
                lax.dot_general(subspace[...], gram[h], NN, precision=HIGHEST, preferred_element_type=F32)
                for h in range(2)
            ],
            axis=1,
        )
        zeros = jnp.zeros_like(product)
        square = lax.dot_general(
            product, jnp.concatenate([product, zeros], axis=0), NT, precision=HIGHEST, preferred_element_type=F32
        )
        inverse = inverse_cholesky(square + identity)
        subspace[...] = lax.dot_general(
            inverse, jnp.concatenate([zeros, product], axis=0), NN, precision=HIGHEST, preferred_element_type=F32
        )
        return carry

    lax.fori_loop(0, ITERS, iterate, 0)
    s_high, s_low = split(subspace[...])
    both = jnp.concatenate([s_high, s_low], axis=0)
    for f in range(high.shape[0]):
        copies[2 * f].wait()
        copies[2 * f + 1].wait()
        first = dot(both, high[f], NN)
        result = first[:k] + first[k:] + dot(s_high, low[f], NN)
        for x in range(core.shape[1]):
            core[f, x] = result[:, 128 * x : 128 * x + 128]


def factor(basis, gram, high, low, cells):
    f, z, columns = high.shape
    k = basis.shape[0]
    vmem = pl.BlockSpec(memory_space=pltpu.VMEM)
    return pl.pallas_call(
        factor_kernel,
        name="factor",
        out_shape=jax.ShapeDtypeStruct((f, cells, k, columns // cells), F32),
        in_specs=[vmem, vmem, pl.BlockSpec(memory_space=pl.ANY), pl.BlockSpec(memory_space=pl.ANY)],
        out_specs=vmem,
        scratch_shapes=[
            pltpu.VMEM((k, z), F32),
            pltpu.VMEM((f, z, columns), BF16),
            pltpu.VMEM((f, z, columns), BF16),
            pltpu.SemaphoreType.DMA((f, 2)),
        ],
        compiler_params=pltpu.CompilerParams(vmem_limit_bytes=48 * 2**20),
    )(basis, gram, high, low)


def local(velocity, initial_basis):
    n_ta, n_af = lax.axis_size("ta"), lax.axis_size("af")
    gram, high, low = regroup(velocity, n_ta, n_af)
    return factor(initial_basis.T, gram, high, low, velocity.shape[2] // n_af)


def solution(mesh):
    placed = (P(None, ("ta", "af"), None, None), P())
    return jax.shard_map(
        local, mesh=mesh, in_specs=placed, out_specs=P("ta", "af", None, None), check_vma=False
    )
```

```python
import functools
import itertools
import random

import jax
import jax.numpy as jnp
from jax import lax
from jax.experimental import pallas as pl
from jax.experimental.pallas import tpu as pltpu
from jax.sharding import PartitionSpec as P

ITERS = 3
MESH = pl.DeviceIdType.MESH
HIGHEST = lax.Precision.HIGHEST
F32, BF16 = jnp.float32, jnp.bfloat16
NN = (((1,), (0,)), ((), ()))
NT = (((1,), (1,)), ((), ()))


def offsets(n_ta, n_af):
    order = [o for o in itertools.product(range(n_ta), range(n_af)) if o != (0, 0)]
    random.Random(0).shuffle(order)
    return order


def split(value):
    high = value.astype(BF16)
    return high, (value - high.astype(F32)).astype(BF16)


def dot(a, b, dims):
    return lax.dot_general(a, b, dims, preferred_element_type=F32)


def exact(a, b, dims):
    return lax.dot_general(a, b, dims, precision=HIGHEST, preferred_element_type=F32)


def wait_bytes(ref, sem):
    pltpu.make_async_copy(ref, ref, sem).wait()


HALVES = (((0, 0), (0, 1), (1, 1), (0, 2), (0, 3)), ((1, 2), (1, 3), (2, 2), (2, 3), (3, 3)))
CHUNKS = ((0, 0, 8), (1, 0, 4), (1, 4, 4))


def regroup_kernel(
    n_ta, n_af, velocity, gathered, high, low, fibres, partial, other, packed, pieces,
    send_sem, recv_sem, own_sem, pair_send, pair_recv, rs_send, rs_recv, ag_send, ag_recv, last_send, last_recv,
):
    n = n_ta * n_af
    ta, af = lax.axis_index("ta"), lax.axis_index("af")
    me = ta * n_af + af
    core, chip = lax.rem(ta, 2), (ta // 2) * n_af + af
    partner = (ta + 1 - 2 * core, af)
    frames, planes, cells = fibres.shape[0], velocity.shape[1], fibres.shape[2]
    order = offsets(n_ta, n_af)
    same_core = [(i, j) for i, j in order if i % 2 == 0]
    tas = [lax.rem(ta + i, n_ta) for i in range(n_ta)]
    afs = [lax.rem(af + j, n_af) for j in range(n_af)]

    def source(t, a, f, x, w):
        return velocity.at[frames * t + f, :, pl.ds(pl.multiple_of(cells * a + x, w), w), :]

    def arrived(f, x, w):
        return fibres.at[f, pl.ds(planes * me, planes), pl.ds(x, w)]

    own = []
    for c, (f, x, w) in enumerate(CHUNKS):
        copy = pltpu.make_async_copy(source(ta, af, f, x, w), arrived(f, x, w), own_sem.at[c])
        copy.start()
        own.append(copy)

    barrier = pltpu.get_barrier_semaphore()
    for i, j in order:
        pl.semaphore_signal(barrier, inc=1, device_id=(tas[i], afs[j]), device_id_type=MESH)
    pl.semaphore_wait(barrier, n - 1)

    def send(src, dst, sems, device):
        copy = pltpu.make_async_remote_copy(
            src_ref=src, dst_ref=dst, send_sem=sems[0], recv_sem=sems[1], device_id=device, device_id_type=MESH
        )
        copy.start()
        return copy

    for c, (f, x, w) in enumerate(CHUNKS):
        for i, j in order:
            send(source(tas[i], afs[j], f, x, w), arrived(f, x, w), (send_sem.at[c], recv_sem.at[c]), (tas[i], afs[j]))

    def others(f, x, w):
        return fibres.at[f, pl.ds(0, planes * (n - 1)), pl.ds(x, w)]

    for c, (f, x, w) in enumerate(CHUNKS):
        own[c].wait()
        wait_bytes(others(f, x, w), recv_sem.at[c])
        for cell in range(x, x + w):
            h, l = split(fibres[f, :, cell, :])
            high[f, :, 128 * cell : 128 * cell + 128] = h
            low[f, :, 128 * cell : 128 * cell + 128] = l
        lanes = slice(128 * x, 128 * x + 128 * w)
        for top, left in ((0, 0), (0, 2), (2, 2)):
            rows, columns = slice(128 * top, 128 * top + 256), slice(128 * left, 128 * left + 256)
            term = (
                dot(high[f, rows, lanes], high[f, columns, lanes], NT)
                + dot(low[f, rows, lanes], high[f, columns, lanes], NT)
                + dot(high[f, rows, lanes], low[f, columns, lanes], NT)
            )
            for s, half in enumerate(HALVES):
                for k, (row, column) in enumerate(half):
                    if row - top in (0, 1) and column - left in (0, 1):
                        u, v = 128 * (row - top), 128 * (column - left)
                        block = term[u : u + 128, v : v + 128]
                        partial[s, k] = block if c == 0 else partial[s, k] + block
    for c, (f, x, w) in enumerate(CHUNKS):
        wait_bytes(others(f, x, w), send_sem.at[c])

    exchange = send(partial.at[1 - core], other, (pair_send, pair_recv), partner)
    exchange.wait_recv()
    for k in range(len(HALVES[0])):
        block = partial[core, k] + other[k]
        packed[:, 2 * k, :] = block[:64]
        packed[:, 2 * k + 1, :] = block[64:]
    for i, j in same_core:
        send(packed.at[(tas[i] // 2) * n_af + afs[j]], pieces.at[chip], (rs_send, rs_recv), (tas[i], afs[j]))
    pieces[chip] = packed[chip]
    rest = pieces.at[pl.ds(0, n // 2 - 1)]
    wait_bytes(rest, rs_recv)
    gathered[core, chip] = jnp.sum(pieces[...], axis=0)
    for i, j in same_core:
        send(gathered.at[core, chip], gathered.at[core, chip], (ag_send, ag_recv), (tas[i], afs[j]))
    exchange.wait_send()
    wait_bytes(rest, rs_send)
    wait_bytes(rest, ag_recv)
    send(gathered.at[core], gathered.at[core], (last_send, last_recv), partner).wait()
    wait_bytes(rest, ag_send)


def regroup(velocity, n_ta, n_af):
    frames, planes, cells, cells_y = velocity.shape
    n = n_ta * n_af
    f, z, x = frames // n_ta, planes * n, cells // n_af
    blocks = len(HALVES[0])
    vmem = pl.BlockSpec(memory_space=pltpu.VMEM)
    dma = pltpu.SemaphoreType.DMA
    return pl.pallas_call(
        functools.partial(regroup_kernel, n_ta, n_af),
        name="regroup",
        out_shape=(
            jax.ShapeDtypeStruct((2, n // 2, 2 * blocks, 128), F32),
            jax.ShapeDtypeStruct((f, z, x * cells_y), BF16),
            jax.ShapeDtypeStruct((f, z, x * cells_y), BF16),
        ),
        in_specs=[pl.BlockSpec(memory_space=pl.ANY)],
        out_specs=(vmem, vmem, vmem),
        scratch_shapes=[
            pltpu.VMEM((f, z, x, cells_y), F32),
            pltpu.VMEM((2, blocks, 128, 128), F32),
            pltpu.VMEM((blocks, 128, 128), F32),
            pltpu.VMEM((n // 2, 2 * blocks, 128), F32),
            pltpu.VMEM((n // 2, 2 * blocks, 128), F32),
            dma((len(CHUNKS),)), dma((len(CHUNKS),)), dma((len(CHUNKS),)),
            dma, dma, dma, dma, dma, dma, dma, dma,
        ],
        compiler_params=pltpu.CompilerParams(
            collective_id=0, has_side_effects=True, vmem_limit_bytes=48 * 2**20
        ),
    )(velocity)


def inverse_cholesky(matrix):
    k, width = matrix.shape
    groups = k // 8
    rows = [matrix[8 * r : 8 * r + 8, :] for r in range(groups)]
    sublane = lax.broadcasted_iota(jnp.int32, (8, width), 0)
    spread = lambda v, c: jnp.broadcast_to(v[c : c + 1, :], (8, width))
    pivots = []
    for g in range(groups):
        columns = [
            [jnp.broadcast_to(rows[r][:, 8 * g + c : 8 * g + c + 1], (8, width)) for r in range(g, groups)]
            for c in range(8)
        ]
        diagonal = None
        for c in range(8):
            pivot = spread(columns[c][0], c)
            diagonal = pivot if c == 0 else jnp.where(sublane == c, pivot, diagonal)
            inverse = pl.reciprocal(pivot, approx=False)
            pivot_row = spread(rows[g], c)
            pivot_columns = {d: spread(columns[d][0], c) for d in range(c + 1, 8)}
            for r in range(g, groups):
                factor = columns[c][r - g] * inverse
                if r == g:
                    factor = jnp.where(sublane > c, factor, 0.0)
                rows[r] = rows[r] - factor * pivot_row
                for d in range(c + 1, 8):
                    columns[d][r - g] = columns[d][r - g] - factor * pivot_columns[d]
        pivots.append(diagonal)
    scaled = []
    for r in range(groups):
        root = lax.rsqrt(pivots[r])
        root = root * (1.5 - 0.5 * (pivots[r] * root) * root)
        scaled.append(rows[r] * root)
    return jnp.concatenate(scaled, axis=0)


def factor_kernel(basis, gathered, high, low, core, subspace, gram):
    for half, blocks in enumerate(HALVES):
        for k, (row, column) in enumerate(blocks):
            block = jnp.concatenate([gathered[half, :, 2 * k, :], gathered[half, :, 2 * k + 1, :]], axis=0)
            rows, columns = slice(128 * row, 128 * row + 128), slice(128 * column, 128 * column + 128)
            gram[rows, columns] = block
            if row != column:
                gram[columns, rows] = block.T
    k, z = basis.shape
    subspace[...] = basis[...]
    row = lax.broadcasted_iota(jnp.int32, (k, 2 * k), 0)
    lane = lax.broadcasted_iota(jnp.int32, (k, 2 * k), 1)
    identity = jnp.where(lane == row + k, 1.0, 0.0).astype(F32)

    def iterate(_, carry):
        product = exact(subspace[...], gram[...], NN)
        zeros = jnp.zeros_like(product)
        square = exact(product, jnp.concatenate([product, zeros], axis=0), NT)
        inverse = inverse_cholesky(square + identity)
        subspace[...] = exact(inverse, jnp.concatenate([zeros, product], axis=0), NN)
        return carry

    lax.fori_loop(0, ITERS, iterate, 0)
    s_high, s_low = split(subspace[...])
    both = jnp.concatenate([s_high, s_low], axis=0)
    for f in range(high.shape[0]):
        first = dot(both, high[f], NN)
        result = first[:k] + first[k:] + dot(s_high, low[f], NN)
        for x in range(core.shape[1]):
            core[f, x] = result[:, 128 * x : 128 * x + 128]


def factor(basis, gathered, high, low, cells):
    f, z, columns = high.shape
    k = basis.shape[0]
    vmem = pl.BlockSpec(memory_space=pltpu.VMEM)
    return pl.pallas_call(
        factor_kernel,
        name="factor",
        out_shape=jax.ShapeDtypeStruct((f, cells, k, columns // cells), F32),
        in_specs=[vmem] * 4,
        out_specs=vmem,
        scratch_shapes=[pltpu.VMEM((k, z), F32), pltpu.VMEM((z, z), F32)],
        compiler_params=pltpu.CompilerParams(vmem_limit_bytes=24 * 2**20),
    )(basis, gathered, high, low)


def local(velocity, initial_basis):
    n_ta, n_af = lax.axis_size("ta"), lax.axis_size("af")
    gram, high, low = regroup(velocity, n_ta, n_af)
    return factor(initial_basis.T, gram, high, low, velocity.shape[2] // n_af)


def solution(mesh):
    placed = (P(None, ("ta", "af"), None, None), P())
    return jax.shard_map(
        local, mesh=mesh, in_specs=placed, out_specs=P("ta", "af", None, None), check_vma=False
    )
```

```python
import functools
import itertools
import math
import random

import jax
import jax.numpy as jnp
from jax import lax
from jax.experimental import pallas as pl
from jax.experimental.pallas import tpu as pltpu
from jax.sharding import PartitionSpec as P

ITERS = 3
MESH = pl.DeviceIdType.MESH
HIGHEST = lax.Precision.HIGHEST
F32, BF16 = jnp.float32, jnp.bfloat16
NN = (((1,), (0,)), ((), ()))
NT = (((1,), (1,)), ((), ()))


def offsets(n_z, n_x, n_y):
    order = [o for o in itertools.product(range(n_z), range(2), range(n_x), range(n_y)) if any(o)]
    random.Random(5).shuffle(order)
    hops = lambda o: sum(min(d, n - d) for d, n in ((o[0], n_z), (o[2], n_x), (o[3], n_y)))
    return sorted(order, key=lambda o: -hops(o))


def split(value):
    high = value.astype(BF16)
    return high, (value - high.astype(F32)).astype(BF16)


def dot(a, b, dims):
    return lax.dot_general(a, b, dims, preferred_element_type=F32)


def exact(a, b, dims):
    return lax.dot_general(a, b, dims, precision=HIGHEST, preferred_element_type=F32)


def wait_bytes(ref, sem):
    pltpu.make_async_copy(ref, ref, sem).wait()


HALVES = (((0, 0), (0, 1), (1, 1), (0, 2), (0, 3)), ((1, 2), (1, 3), (2, 2), (2, 3), (3, 3)))
CHUNKS = ((0, 0, 8), (1, 0, 6), (1, 6, 2))


def regroup_kernel(
    n_ta, n_af, velocity, gathered, high, low, fibres, partial, other, packed, pieces,
    send_sem, recv_sem, own_sem, pair_send, pair_recv, rs_send, rs_recv, ag_send, ag_recv, last_send, last_recv,
):
    n = n_ta * n_af
    ta, af = lax.axis_index("ta"), lax.axis_index("af")
    me = ta * n_af + af
    core, chip = lax.rem(ta, 2), (ta // 2) * n_af + af
    partner = (ta + 1 - 2 * core, af)
    frames, planes, cells = fibres.shape[0], velocity.shape[1], fibres.shape[2]
    n_z, side = n_ta // 2, math.isqrt(n_af)
    z, x_, y_ = ta // 2, af // side, lax.rem(af, side)
    zs = [lax.rem(z + d, n_z) for d in range(n_z)]
    tas = [[2 * zs[d] + core, 2 * zs[d] + 1 - core] for d in range(n_z)]
    xs = [side * lax.rem(x_ + d, side) for d in range(side)]
    ys = [lax.rem(y_ + d, side) for d in range(side)]
    afs = [[xs[i] + ys[j] for j in range(side)] for i in range(side)]
    order = [(tas[d][c], afs[i][j]) for d, c, i, j in offsets(n_z, side, side)]
    same_core = [(tas[d][0], afs[i][j]) for d, c, i, j in offsets(n_z, side, side) if c == 0]

    def source(t, a, f, x, w):
        return velocity.at[frames * t + f, :, pl.ds(pl.multiple_of(cells * a + x, 2), w), :]

    def arrived(f, x, w):
        return fibres.at[f, pl.ds(planes * me, planes), pl.ds(x, w)]

    own = []
    for c, (f, x, w) in enumerate(CHUNKS):
        copy = pltpu.make_async_copy(source(ta, af, f, x, w), arrived(f, x, w), own_sem.at[c])
        copy.start()
        own.append(copy)

    barrier = pltpu.get_barrier_semaphore()
    for device in order:
        pl.semaphore_signal(barrier, inc=1, device_id=device, device_id_type=MESH)
    pl.semaphore_wait(barrier, n - 1)

    def send(src, dst, sems, device):
        copy = pltpu.make_async_remote_copy(
            src_ref=src, dst_ref=dst, send_sem=sems[0], recv_sem=sems[1], device_id=device, device_id_type=MESH
        )
        copy.start()
        return copy

    for c, (f, x, w) in enumerate(CHUNKS):
        for t, a in order:
            send(source(t, a, f, x, w), arrived(f, x, w), (send_sem.at[c], recv_sem.at[c]), (t, a))

    def others(f, x, w):
        return fibres.at[f, pl.ds(0, planes * (n - 1)), pl.ds(x, w)]

    for c, (f, x, w) in enumerate(CHUNKS):
        own[c].wait()
        wait_bytes(others(f, x, w), recv_sem.at[c])
        for cell in range(x, x + w):
            h, l = split(fibres[f, :, cell, :])
            high[f, :, 128 * cell : 128 * cell + 128] = h
            low[f, :, 128 * cell : 128 * cell + 128] = l
        lanes = slice(128 * x, 128 * x + 128 * w)
        for top, left in ((0, 0), (0, 2), (2, 2)):
            rows, columns = slice(128 * top, 128 * top + 256), slice(128 * left, 128 * left + 256)
            term = (
                dot(high[f, rows, lanes], high[f, columns, lanes], NT)
                + dot(low[f, rows, lanes], high[f, columns, lanes], NT)
                + dot(high[f, rows, lanes], low[f, columns, lanes], NT)
            )
            for s, half in enumerate(HALVES):
                for k, (row, column) in enumerate(half):
                    if row - top in (0, 1) and column - left in (0, 1):
                        u, v = 128 * (row - top), 128 * (column - left)
                        block = term[u : u + 128, v : v + 128]
                        partial[s, k] = block if c == 0 else partial[s, k] + block
    for c, (f, x, w) in enumerate(CHUNKS):
        wait_bytes(others(f, x, w), send_sem.at[c])

    exchange = send(partial.at[1 - core], other, (pair_send, pair_recv), partner)
    exchange.wait_recv()
    for k in range(len(HALVES[0])):
        block = partial[core, k] + other[k]
        packed[:, 2 * k, :] = block[:64]
        packed[:, 2 * k + 1, :] = block[64:]
    for t, a in same_core:
        send(packed.at[(t // 2) * n_af + a], pieces.at[chip], (rs_send, rs_recv), (t, a))
    pieces[chip] = packed[chip]
    rest = pieces.at[pl.ds(0, n // 2 - 1)]
    wait_bytes(rest, rs_recv)
    gathered[core, chip] = jnp.sum(pieces[...], axis=0)
    for device in same_core:
        send(gathered.at[core, chip], gathered.at[core, chip], (ag_send, ag_recv), device)
    exchange.wait_send()
    wait_bytes(rest, rs_send)
    wait_bytes(rest, ag_recv)
    send(gathered.at[core], gathered.at[core], (last_send, last_recv), partner).wait()
    wait_bytes(rest, ag_send)


def regroup(velocity, n_ta, n_af):
    frames, planes, cells, cells_y = velocity.shape
    n = n_ta * n_af
    f, z, x = frames // n_ta, planes * n, cells // n_af
    blocks = len(HALVES[0])
    vmem = pl.BlockSpec(memory_space=pltpu.VMEM)
    dma = pltpu.SemaphoreType.DMA
    return pl.pallas_call(
        functools.partial(regroup_kernel, n_ta, n_af),
        name="regroup",
        out_shape=(
            jax.ShapeDtypeStruct((2, n // 2, 2 * blocks, 128), F32),
            jax.ShapeDtypeStruct((f, z, x * cells_y), BF16),
            jax.ShapeDtypeStruct((f, z, x * cells_y), BF16),
        ),
        in_specs=[pl.BlockSpec(memory_space=pl.ANY)],
        out_specs=(vmem, vmem, vmem),
        scratch_shapes=[
            pltpu.VMEM((f, z, x, cells_y), F32),
            pltpu.VMEM((2, blocks, 128, 128), F32),
            pltpu.VMEM((blocks, 128, 128), F32),
            pltpu.VMEM((n // 2, 2 * blocks, 128), F32),
            pltpu.VMEM((n // 2, 2 * blocks, 128), F32),
            dma((len(CHUNKS),)), dma((len(CHUNKS),)), dma((len(CHUNKS),)),
            dma, dma, dma, dma, dma, dma, dma, dma,
        ],
        compiler_params=pltpu.CompilerParams(
            collective_id=0, has_side_effects=True, vmem_limit_bytes=48 * 2**20
        ),
    )(velocity)


def inverse_cholesky(matrix):
    k, width = matrix.shape
    groups = k // 8
    rows = [matrix[8 * r : 8 * r + 8, :] for r in range(groups)]
    sublane = lax.broadcasted_iota(jnp.int32, (8, width), 0)
    spread = lambda v, c: jnp.broadcast_to(v[c : c + 1, :], (8, width))
    pivots = []
    for g in range(groups):
        columns = [
            [jnp.broadcast_to(rows[r][:, 8 * g + c : 8 * g + c + 1], (8, width)) for r in range(g, groups)]
            for c in range(8)
        ]
        diagonal = None
        for c in range(8):
            pivot = spread(columns[c][0], c)
            diagonal = pivot if c == 0 else jnp.where(sublane == c, pivot, diagonal)
            inverse = pl.reciprocal(pivot, approx=False)
            pivot_row = spread(rows[g], c)
            pivot_columns = {d: spread(columns[d][0], c) for d in range(c + 1, 8)}
            for r in range(g, groups):
                factor = columns[c][r - g] * inverse
                if r == g:
                    factor = jnp.where(sublane > c, factor, 0.0)
                rows[r] = rows[r] - factor * pivot_row
                for d in range(c + 1, 8):
                    columns[d][r - g] = columns[d][r - g] - factor * pivot_columns[d]
        pivots.append(diagonal)
    scaled = []
    for r in range(groups):
        root = lax.rsqrt(pivots[r])
        root = root * (1.5 - 0.5 * (pivots[r] * root) * root)
        scaled.append(rows[r] * root)
    return jnp.concatenate(scaled, axis=0)


def factor_kernel(basis, gathered, high, low, core, subspace, gram):
    for half, blocks in enumerate(HALVES):
        for k, (row, column) in enumerate(blocks):
            block = jnp.concatenate([gathered[half, :, 2 * k, :], gathered[half, :, 2 * k + 1, :]], axis=0)
            rows, columns = slice(128 * row, 128 * row + 128), slice(128 * column, 128 * column + 128)
            gram[rows, columns] = block
            if row != column:
                gram[columns, rows] = block.T
    k, z = basis.shape
    subspace[...] = basis[...]
    row = lax.broadcasted_iota(jnp.int32, (k, 2 * k), 0)
    lane = lax.broadcasted_iota(jnp.int32, (k, 2 * k), 1)
    identity = jnp.where(lane == row + k, 1.0, 0.0).astype(F32)

    def iterate():
        product = exact(subspace[...], gram[...], NN)
        zeros = jnp.zeros_like(product)
        square = exact(product, jnp.concatenate([product, zeros], axis=0), NT)
        inverse = inverse_cholesky(square + identity)
        subspace[...] = exact(inverse, jnp.concatenate([zeros, product], axis=0), NN)

    for _ in range(ITERS):
        iterate()
    s_high, s_low = split(subspace[...])
    both = jnp.concatenate([s_high, s_low], axis=0)
    for f in range(high.shape[0]):
        first = dot(both, high[f], NN)
        result = first[:k] + first[k:] + dot(s_high, low[f], NN)
        for x in range(core.shape[1]):
            core[f, x] = result[:, 128 * x : 128 * x + 128]


def factor(basis, gathered, high, low, cells):
    f, z, columns = high.shape
    k = basis.shape[0]
    vmem = pl.BlockSpec(memory_space=pltpu.VMEM)
    return pl.pallas_call(
        factor_kernel,
        name="factor",
        out_shape=jax.ShapeDtypeStruct((f, cells, k, columns // cells), F32),
        in_specs=[vmem] * 4,
        out_specs=vmem,
        scratch_shapes=[pltpu.VMEM((k, z), F32), pltpu.VMEM((z, z), F32)],
        compiler_params=pltpu.CompilerParams(vmem_limit_bytes=24 * 2**20),
    )(basis, gathered, high, low)


def local(velocity, initial_basis):
    n_ta, n_af = lax.axis_size("ta"), lax.axis_size("af")
    gram, high, low = regroup(velocity, n_ta, n_af)
    return factor(initial_basis.T, gram, high, low, velocity.shape[2] // n_af)


def solution(mesh):
    placed = (P(None, ("ta", "af"), None, None), P())
    return jax.shard_map(
        local, mesh=mesh, in_specs=placed, out_specs=P("ta", "af", None, None), check_vma=False
    )
```

```python
import functools
import itertools
import math
import random

import jax
import jax.numpy as jnp
from jax import lax
from jax.experimental import pallas as pl
from jax.experimental.pallas import tpu as pltpu
from jax.sharding import PartitionSpec as P

ITERS = 3
MESH = pl.DeviceIdType.MESH
HIGHEST = lax.Precision.HIGHEST
F32, BF16 = jnp.float32, jnp.bfloat16
NN = (((1,), (0,)), ((), ()))
NT = (((1,), (1,)), ((), ()))


def offsets(n_z, n_x, n_y):
    order = [o for o in itertools.product(range(n_z), range(2), range(n_x), range(n_y)) if any(o)]
    random.Random(5).shuffle(order)
    hops = lambda o: sum(min(d, n - d) for d, n in ((o[0], n_z), (o[2], n_x), (o[3], n_y)))
    return sorted(order, key=lambda o: -hops(o))


def split(value):
    high = value.astype(BF16)
    return high, (value - high.astype(F32)).astype(BF16)


def dot(a, b, dims):
    return lax.dot_general(a, b, dims, preferred_element_type=F32)


def exact(a, b, dims):
    return lax.dot_general(a, b, dims, precision=HIGHEST, preferred_element_type=F32)


def wait_bytes(ref, sem):
    pltpu.make_async_copy(ref, ref, sem).wait()


HALVES = (((0, 0), (0, 1), (1, 1), (0, 2), (0, 3)), ((1, 2), (1, 3), (2, 2), (2, 3), (3, 3)))
CHUNKS = ((0, 0, 8), (1, 0, 4), (1, 4, 4))


def regroup_kernel(
    n_ta, n_af, velocity, gathered, high, low, fibres, partial, other, packed, pieces,
    send_sem, recv_sem, own_sem, pair_send, pair_recv, rs_send, rs_recv, ag_send, ag_recv, last_send, last_recv,
):
    n = n_ta * n_af
    ta, af = lax.axis_index("ta"), lax.axis_index("af")
    me = ta * n_af + af
    core, chip = lax.rem(ta, 2), (ta // 2) * n_af + af
    partner = (ta + 1 - 2 * core, af)
    frames, planes, cells = fibres.shape[0], velocity.shape[1], fibres.shape[2]
    n_z, side = n_ta // 2, math.isqrt(n_af)
    z, x_, y_ = ta // 2, af // side, lax.rem(af, side)
    zs = [lax.rem(z + d, n_z) for d in range(n_z)]
    tas = [[2 * zs[d] + core, 2 * zs[d] + 1 - core] for d in range(n_z)]
    xs = [side * lax.rem(x_ + d, side) for d in range(side)]
    ys = [lax.rem(y_ + d, side) for d in range(side)]
    afs = [[xs[i] + ys[j] for j in range(side)] for i in range(side)]
    order = [(tas[d][c], afs[i][j]) for d, c, i, j in offsets(n_z, side, side)]
    same_core = [(tas[d][0], afs[i][j]) for d, c, i, j in offsets(n_z, side, side) if c == 0]

    def source(t, a, f, x, w):
        return velocity.at[frames * t + f, :, pl.ds(pl.multiple_of(cells * a + x, 2), w), :]

    def arrived(f, x, w):
        return fibres.at[f, pl.ds(planes * me, planes), pl.ds(x, w)]

    own = []
    for c, (f, x, w) in enumerate(CHUNKS):
        copy = pltpu.make_async_copy(source(ta, af, f, x, w), arrived(f, x, w), own_sem.at[c])
        copy.start()
        own.append(copy)

    barrier = pltpu.get_barrier_semaphore()
    for device in order:
        pl.semaphore_signal(barrier, inc=1, device_id=device, device_id_type=MESH)
    pl.semaphore_wait(barrier, n - 1)

    def send(src, dst, sems, device):
        copy = pltpu.make_async_remote_copy(
            src_ref=src, dst_ref=dst, send_sem=sems[0], recv_sem=sems[1], device_id=device, device_id_type=MESH
        )
        copy.start()
        return copy

    for c, (f, x, w) in enumerate(CHUNKS):
        for t, a in order:
            send(source(t, a, f, x, w), arrived(f, x, w), (send_sem.at[c], recv_sem.at[c]), (t, a))

    def others(f, x, w):
        return fibres.at[f, pl.ds(0, planes * (n - 1)), pl.ds(x, w)]

    for c, (f, x, w) in enumerate(CHUNKS):
        own[c].wait()
        wait_bytes(others(f, x, w), recv_sem.at[c])
        for cell in range(x, x + w):
            h, l = split(fibres[f, :, cell, :])
            high[f, :, 128 * cell : 128 * cell + 128] = h
            low[f, :, 128 * cell : 128 * cell + 128] = l
        lanes = slice(128 * x, 128 * x + 128 * w)
        for top, left in ((0, 0), (0, 2), (2, 2)):
            rows, columns = slice(128 * top, 128 * top + 256), slice(128 * left, 128 * left + 256)
            term = (
                dot(high[f, rows, lanes], high[f, columns, lanes], NT)
                + dot(low[f, rows, lanes], high[f, columns, lanes], NT)
                + dot(high[f, rows, lanes], low[f, columns, lanes], NT)
            )
            for s, half in enumerate(HALVES):
                for k, (row, column) in enumerate(half):
                    if row - top in (0, 1) and column - left in (0, 1):
                        u, v = 128 * (row - top), 128 * (column - left)
                        block = term[u : u + 128, v : v + 128]
                        partial[s, k] = block if c == 0 else partial[s, k] + block
    for c, (f, x, w) in enumerate(CHUNKS):
        wait_bytes(others(f, x, w), send_sem.at[c])

    exchange = send(partial.at[1 - core], other, (pair_send, pair_recv), partner)
    exchange.wait_recv()
    for k in range(len(HALVES[0])):
        block = partial[core, k] + other[k]
        packed[:, 2 * k, :] = block[:64]
        packed[:, 2 * k + 1, :] = block[64:]
    for t, a in same_core:
        send(packed.at[(t // 2) * n_af + a], pieces.at[chip], (rs_send, rs_recv), (t, a))
    pieces[chip] = packed[chip]
    rest = pieces.at[pl.ds(0, n // 2 - 1)]
    wait_bytes(rest, rs_recv)
    gathered[core, chip] = jnp.sum(pieces[...], axis=0)
    for device in same_core:
        send(gathered.at[core, chip], gathered.at[core, chip], (ag_send, ag_recv), device)
    exchange.wait_send()
    wait_bytes(rest, rs_send)
    wait_bytes(rest, ag_recv)
    send(gathered.at[core], gathered.at[core], (last_send, last_recv), partner).wait()
    wait_bytes(rest, ag_send)


def regroup(velocity, n_ta, n_af):
    frames, planes, cells, cells_y = velocity.shape
    n = n_ta * n_af
    f, z, x = frames // n_ta, planes * n, cells // n_af
    blocks = len(HALVES[0])
    vmem = pl.BlockSpec(memory_space=pltpu.VMEM)
    dma = pltpu.SemaphoreType.DMA
    return pl.pallas_call(
        functools.partial(regroup_kernel, n_ta, n_af),
        name="regroup",
        out_shape=(
            jax.ShapeDtypeStruct((2, n // 2, 2 * blocks, 128), F32),
            jax.ShapeDtypeStruct((f, z, x * cells_y), BF16),
            jax.ShapeDtypeStruct((f, z, x * cells_y), BF16),
        ),
        in_specs=[pl.BlockSpec(memory_space=pl.ANY)],
        out_specs=(vmem, vmem, vmem),
        scratch_shapes=[
            pltpu.VMEM((f, z, x, cells_y), F32),
            pltpu.VMEM((2, blocks, 128, 128), F32),
            pltpu.VMEM((blocks, 128, 128), F32),
            pltpu.VMEM((n // 2, 2 * blocks, 128), F32),
            pltpu.VMEM((n // 2, 2 * blocks, 128), F32),
            dma((len(CHUNKS),)), dma((len(CHUNKS),)), dma((len(CHUNKS),)),
            dma, dma, dma, dma, dma, dma, dma, dma,
        ],
        compiler_params=pltpu.CompilerParams(
            collective_id=0, has_side_effects=True, vmem_limit_bytes=48 * 2**20
        ),
    )(velocity)


def inverse_cholesky(matrix):
    k, width = matrix.shape
    groups = k // 8
    rows = [matrix[8 * r : 8 * r + 8, :] for r in range(groups)]
    sublane = lax.broadcasted_iota(jnp.int32, (8, width), 0)
    spread = lambda v, c: jnp.broadcast_to(v[c : c + 1, :], (8, width))
    lane = lambda v, c: jnp.take_along_axis(v, jnp.full((8, width), c, jnp.int32), axis=1)
    pivots = []
    ahead = {}
    for g in range(groups):
        columns = [{r: ahead[d, r] if (d, r) in ahead else lane(rows[r], 8 * g + d) for r in range(g, groups)} for d in range(8)]
        late = range(g + 1, min(g + 1 + 1, groups))
        ahead = {(d, r): lane(rows[r], 8 * g + 8 + d) for r in late for d in range(8)}
        diagonal = None
        for c in range(8):
            pivot = spread(columns[c][g], c)
            diagonal = pivot if c == 0 else jnp.where(sublane == c, pivot, diagonal)
            inverse = 1.0 / pivot
            pivot_row = spread(rows[g], c)
            inside = {d: spread(columns[d][g], c) for d in range(c + 1, 8)}
            outside = {d: spread(columns[c][g + 1], d) for d in range(8)} if g + 1 < groups else {}
            for r in range(g, groups):
                factor = columns[c][r] * inverse
                if r == g:
                    factor = jnp.where(sublane > c, factor, 0.0)
                for d in range(c + 1, 8):
                    columns[d][r] = columns[d][r] - factor * inside[d]
                if r in late:
                    for d in range(8):
                        ahead[d, r] = ahead[d, r] - factor * outside[d]
                rows[r] = rows[r] - factor * pivot_row
        pivots.append(diagonal)
    scaled = []
    for r in range(groups):
        root = lax.rsqrt(pivots[r])
        root = root * (1.5 - 0.5 * (pivots[r] * root) * root)
        scaled.append(rows[r] * root)
    return jnp.concatenate(scaled, axis=0)


def factor_kernel(basis, gathered, high, low, core, subspace, gram, g1, g2, g3):
    for half, blocks in enumerate(HALVES):
        for k, (row, column) in enumerate(blocks):
            block = jnp.concatenate([gathered[half, :, 2 * k, :], gathered[half, :, 2 * k + 1, :]], axis=0)
            rows, columns = slice(128 * row, 128 * row + 128), slice(128 * column, 128 * column + 128)
            gram[rows, columns] = block
            if row != column:
                gram[columns, rows] = block.T
    k, z = basis.shape
    subspace[...] = basis[...]
    h, l = split(gram[...])
    g1[...] = h
    g2[...] = l
    g3[...] = (gram[...] - h.astype(F32) - l.astype(F32)).astype(BF16)
    row = lax.broadcasted_iota(jnp.int32, (k, 2 * k), 0)
    lane = lax.broadcasted_iota(jnp.int32, (k, 2 * k), 1)
    identity = jnp.where(lane == row + k, 1.0, 0.0).astype(F32)

    def iterate():
        s1, s2 = split(subspace[...])
        s3 = (subspace[...] - s1.astype(F32) - s2.astype(F32)).astype(BF16)
        t1 = dot(jnp.concatenate([s1, s2, s3], axis=0), g1[...], NN)
        t2 = dot(jnp.concatenate([s1, s2], axis=0), g2[...], NN)
        product = (t2[k:] + (t1[2 * k:] + dot(s1, g3[...], NN))) + (t1[k:2 * k] + t2[:k]) + t1[:k]
        zeros = jnp.zeros_like(product)
        square = exact(product, jnp.concatenate([product, zeros], axis=0), NT)
        inverse = inverse_cholesky(square + identity)
        subspace[...] = exact(inverse, jnp.concatenate([zeros, product], axis=0), NN)

    for _ in range(ITERS):
        iterate()
    s_high, s_low = split(subspace[...])
    both = jnp.concatenate([s_high, s_low], axis=0)
    for f in range(high.shape[0]):
        first = dot(both, high[f], NN)
        result = first[:k] + first[k:] + dot(s_high, low[f], NN)
        for x in range(core.shape[1]):
            core[f, x] = result[:, 128 * x : 128 * x + 128]


def factor(basis, gathered, high, low, cells):
    f, z, columns = high.shape
    k = basis.shape[0]
    vmem = pl.BlockSpec(memory_space=pltpu.VMEM)
    return pl.pallas_call(
        factor_kernel,
        name="factor",
        out_shape=jax.ShapeDtypeStruct((f, cells, k, columns // cells), F32),
        in_specs=[vmem] * 4,
        out_specs=vmem,
        scratch_shapes=[pltpu.VMEM((k, z), F32), pltpu.VMEM((z, z), F32)] + [pltpu.VMEM((z, z), BF16)] * 3,
        compiler_params=pltpu.CompilerParams(vmem_limit_bytes=24 * 2**20),
    )(basis, gathered, high, low)


def local(velocity, initial_basis):
    n_ta, n_af = lax.axis_size("ta"), lax.axis_size("af")
    gram, high, low = regroup(velocity, n_ta, n_af)
    return factor(initial_basis.T, gram, high, low, velocity.shape[2] // n_af)


def solution(mesh):
    placed = (P(None, ("ta", "af"), None, None), P())
    return jax.shard_map(
        local, mesh=mesh, in_specs=placed, out_specs=P("ta", "af", None, None), check_vma=False
    )
```

```python
import functools
import itertools
import math
import random

import jax
import jax.numpy as jnp
from jax import lax
from jax.experimental import pallas as pl
from jax.experimental.pallas import tpu as pltpu
from jax.sharding import PartitionSpec as P

ITERS = 3
MESH = pl.DeviceIdType.MESH
HIGHEST = lax.Precision.HIGHEST
F32, BF16 = jnp.float32, jnp.bfloat16
NN = (((1,), (0,)), ((), ()))
NT = (((1,), (1,)), ((), ()))


def offsets(n_z, n_x, n_y):
    order = [o for o in itertools.product(range(n_z), range(2), range(n_x), range(n_y)) if any(o)]
    random.Random(5).shuffle(order)
    hops = lambda o: sum(min(d, n - d) for d, n in ((o[0], n_z), (o[2], n_x), (o[3], n_y)))
    return sorted(order, key=lambda o: -hops(o))


def split(value):
    high = value.astype(BF16)
    return high, (value - high.astype(F32)).astype(BF16)


def dot(a, b, dims):
    return lax.dot_general(a, b, dims, preferred_element_type=F32)


def exact(a, b, dims):
    return lax.dot_general(a, b, dims, precision=HIGHEST, preferred_element_type=F32)


def wait_bytes(ref, sem):
    pltpu.make_async_copy(ref, ref, sem).wait()


HALVES = (((0, 0), (0, 1), (1, 1), (0, 2), (0, 3)), ((1, 2), (1, 3), (2, 2), (2, 3), (3, 3)))
PAD = 16
CHUNKS = ((0, 0, 8), (1, 0, 4), (1, 4, 2), (1, 6, 2))


def regroup_kernel(
    n_ta, n_af, velocity, gathered, high, low, fibres, partial, other, packed, pieces,
    send_sem, recv_sem, own_sem, pair_send, pair_recv, rs_send, rs_recv, ag_send, ag_recv, last_send, last_recv,
):
    n = n_ta * n_af
    ta, af = lax.axis_index("ta"), lax.axis_index("af")
    me = ta * n_af + af
    core, chip = lax.rem(ta, 2), (ta // 2) * n_af + af
    partner = (ta + 1 - 2 * core, af)
    frames, planes, cells = fibres.shape[0], velocity.shape[1], fibres.shape[2]
    n_z, side = n_ta // 2, math.isqrt(n_af)
    z, x_, y_ = ta // 2, af // side, lax.rem(af, side)
    zs = [lax.rem(z + d, n_z) for d in range(n_z)]
    tas = [[2 * zs[d] + core, 2 * zs[d] + 1 - core] for d in range(n_z)]
    xs = [side * lax.rem(x_ + d, side) for d in range(side)]
    ys = [lax.rem(y_ + d, side) for d in range(side)]
    afs = [[xs[i] + ys[j] for j in range(side)] for i in range(side)]
    order = [(tas[d][c], afs[i][j]) for d, c, i, j in offsets(n_z, side, side)]
    same_core = [(tas[d][0], afs[i][j]) for d, c, i, j in offsets(n_z, side, side) if c == 0]

    def source(t, a, f, x, w):
        return velocity.at[frames * t + f, :, pl.ds(pl.multiple_of(cells * a + x, 2), w), :]

    def arrived(f, x, w):
        return fibres.at[f, pl.ds(planes * me, planes), pl.ds(x, w)]

    own = []
    for c, (f, x, w) in enumerate(CHUNKS):
        copy = pltpu.make_async_copy(source(ta, af, f, x, w), arrived(f, x, w), own_sem.at[c])
        copy.start()
        own.append(copy)

    barrier = pltpu.get_barrier_semaphore()
    for device in order:
        pl.semaphore_signal(barrier, inc=1, device_id=device, device_id_type=MESH)
    pl.semaphore_wait(barrier, n - 1)

    def send(src, dst, sems, device):
        copy = pltpu.make_async_remote_copy(
            src_ref=src, dst_ref=dst, send_sem=sems[0], recv_sem=sems[1], device_id=device, device_id_type=MESH
        )
        copy.start()
        return copy

    for c, (f, x, w) in enumerate(CHUNKS):
        for t, a in order:
            send(source(t, a, f, x, w), arrived(f, x, w), (send_sem.at[c], recv_sem.at[c]), (t, a))

    flat = fibres.reshape(frames, planes * n * cells, 128)

    def others(f, x, w):
        return fibres.at[f, pl.ds(0, planes * (n - 1)), pl.ds(x, w)]

    for c, (f, x, w) in enumerate(CHUNKS):
        own[c].wait()
        wait_bytes(others(f, x, w), recv_sem.at[c])
        for cell in range(x, x + w):
            h, l = split(flat[f, pl.ds(cell, planes * n, stride=cells), :])
            high[f, :, 128 * cell : 128 * cell + 128] = h
            low[f, :, 128 * cell : 128 * cell + 128] = l
        lanes = slice(128 * x, 128 * x + 128 * w)
        for top, left in ((0, 0), (0, 2), (2, 2)):
            rows, columns = slice(128 * top, 128 * top + 256), slice(128 * left, 128 * left + 256)
            term = (
                dot(high[f, rows, lanes], high[f, columns, lanes], NT)
                + dot(low[f, rows, lanes], high[f, columns, lanes], NT)
                + dot(high[f, rows, lanes], low[f, columns, lanes], NT)
            )
            for s, half in enumerate(HALVES):
                for k, (row, column) in enumerate(half):
                    if row - top in (0, 1) and column - left in (0, 1):
                        u, v = 128 * (row - top), 128 * (column - left)
                        block = term[u : u + 128, v : v + 128]
                        partial[s, k] = block if c == 0 else partial[s, k] + block
    for c, (f, x, w) in enumerate(CHUNKS):
        wait_bytes(others(f, x, w), send_sem.at[c])

    used = pl.ds(0, 2 * len(HALVES[0]))
    exchange = send(partial.at[1 - core], other, (pair_send, pair_recv), partner)
    exchange.wait_recv()
    flat_packed = packed.reshape(n // 2 * PAD, 128)
    for k in range(len(HALVES[0])):
        block = partial[core, k] + other[k]
        for part in range(2):
            flat_packed[pl.ds(2 * k + part, n // 2, stride=PAD), :] = block[64 * part : 64 * part + 64]
    for t, a in same_core:
        send(packed.at[(t // 2) * n_af + a, used], pieces.at[chip, used], (rs_send, rs_recv), (t, a))
    pieces[chip] = packed[chip]
    rest = pieces.at[pl.ds(0, n // 2 - 1), used]
    wait_bytes(rest, rs_recv)
    gathered[core, chip, used] = jnp.sum(pieces[:, used, :], axis=0)
    mine = gathered.at[core, chip, used]
    for device in same_core:
        send(mine, mine, (ag_send, ag_recv), device)
    exchange.wait_send()
    wait_bytes(rest, rs_send)
    wait_bytes(rest, ag_recv)
    half = gathered.at[core, :, used]
    send(half, half, (last_send, last_recv), partner).wait()
    wait_bytes(rest, ag_send)


def regroup(velocity, n_ta, n_af):
    frames, planes, cells, cells_y = velocity.shape
    n = n_ta * n_af
    f, z, x = frames // n_ta, planes * n, cells // n_af
    blocks = len(HALVES[0])
    vmem = pl.BlockSpec(memory_space=pltpu.VMEM)
    dma = pltpu.SemaphoreType.DMA
    return pl.pallas_call(
        functools.partial(regroup_kernel, n_ta, n_af),
        name="regroup",
        out_shape=(
            jax.ShapeDtypeStruct((2, n // 2, PAD, 128), F32),
            jax.ShapeDtypeStruct((f, z, x * cells_y), BF16),
            jax.ShapeDtypeStruct((f, z, x * cells_y), BF16),
        ),
        in_specs=[pl.BlockSpec(memory_space=pl.ANY)],
        out_specs=(vmem, vmem, vmem),
        scratch_shapes=[
            pltpu.VMEM((f, z, x, cells_y), F32),
            pltpu.VMEM((2, blocks, 128, 128), F32),
            pltpu.VMEM((blocks, 128, 128), F32),
            pltpu.VMEM((n // 2, PAD, 128), F32),
            pltpu.VMEM((n // 2, PAD, 128), F32),
            dma((len(CHUNKS),)), dma((len(CHUNKS),)), dma((len(CHUNKS),)),
            dma, dma, dma, dma, dma, dma, dma, dma,
        ],
        compiler_params=pltpu.CompilerParams(
            collective_id=0, has_side_effects=True, vmem_limit_bytes=48 * 2**20
        ),
    )(velocity)


def inverse_cholesky(matrix):
    k, width = matrix.shape
    groups = k // 8
    rows = [matrix[8 * r : 8 * r + 8, :] for r in range(groups)]
    sublane = lax.broadcasted_iota(jnp.int32, (8, width), 0)
    spread = lambda v, c: jnp.broadcast_to(v[c : c + 1, :], (8, width))
    lane = lambda v, c: jnp.take_along_axis(v, jnp.full((8, width), c, jnp.int32), axis=1)
    pivots = []
    ahead = {}
    for g in range(groups):
        columns = [{r: ahead[d, r] if (d, r) in ahead else lane(rows[r], 8 * g + d) for r in range(g, groups)} for d in range(8)]
        late = range(g + 1, min(g + 1 + 1, groups))
        ahead = {(d, r): lane(rows[r], 8 * g + 8 + d) for r in late for d in range(8)}
        diagonal = None
        for c in range(8):
            pivot = spread(columns[c][g], c)
            diagonal = pivot if c == 0 else jnp.where(sublane == c, pivot, diagonal)
            inverse = 1.0 / pivot
            pivot_row = spread(rows[g], c)
            inside = {d: spread(columns[d][g], c) for d in range(c + 1, 8)}
            outside = {d: spread(columns[c][g + 1], d) for d in range(8)} if g + 1 < groups else {}
            for r in range(g, groups):
                factor = columns[c][r] * inverse
                if r == g:
                    factor = jnp.where(sublane > c, factor, 0.0)
                for d in range(c + 1, 8):
                    columns[d][r] = columns[d][r] - factor * inside[d]
                if r in late:
                    for d in range(8):
                        ahead[d, r] = ahead[d, r] - factor * outside[d]
                rows[r] = rows[r] - factor * pivot_row
        pivots.append(diagonal)
    scaled = []
    for r in range(groups):
        root = lax.rsqrt(pivots[r])
        root = root * (1.5 - 0.5 * (pivots[r] * root) * root)
        scaled.append(rows[r] * root)
    return jnp.concatenate(scaled, axis=0)


def factor_kernel(basis, gathered, high, low, core, subspace, gram, g1, g2, g3):
    flat = gathered.reshape(2, gathered.shape[1] * PAD, 128)
    for half, blocks in enumerate(HALVES):
        for k, (row, column) in enumerate(blocks):
            block = jnp.concatenate([flat[half, pl.ds(2 * k + p, 64, stride=PAD), :] for p in range(2)], axis=0)
            rows, columns = slice(128 * row, 128 * row + 128), slice(128 * column, 128 * column + 128)
            gram[rows, columns] = block
            if row != column:
                gram[columns, rows] = block.T
    k, z = basis.shape
    subspace[...] = basis[...]
    h, l = split(gram[...])
    g1[...] = h
    g2[...] = l
    g3[...] = (gram[...] - h.astype(F32) - l.astype(F32)).astype(BF16)
    row = lax.broadcasted_iota(jnp.int32, (k, 2 * k), 0)
    lane = lax.broadcasted_iota(jnp.int32, (k, 2 * k), 1)
    identity = jnp.where(lane == row + k, 1.0, 0.0).astype(F32)

    def iterate():
        s1, s2 = split(subspace[...])
        s3 = (subspace[...] - s1.astype(F32) - s2.astype(F32)).astype(BF16)
        t1 = dot(jnp.concatenate([s1, s2, s3], axis=0), g1[...], NN)
        t2 = dot(jnp.concatenate([s1, s2], axis=0), g2[...], NN)
        product = (t2[k:] + (t1[2 * k:] + dot(s1, g3[...], NN))) + (t1[k:2 * k] + t2[:k]) + t1[:k]
        zeros = jnp.zeros_like(product)
        square = exact(product, jnp.concatenate([product, zeros], axis=0), NT)
        inverse = inverse_cholesky(square + identity)
        subspace[...] = exact(inverse, jnp.concatenate([zeros, product], axis=0), NN)

    for _ in range(ITERS):
        iterate()
    s_high, s_low = split(subspace[...])
    both = jnp.concatenate([s_high, s_low], axis=0)
    for f in range(high.shape[0]):
        first = dot(both, high[f], NN)
        result = first[:k] + first[k:] + dot(s_high, low[f], NN)
        for x in range(core.shape[1]):
            core[f, x] = result[:, 128 * x : 128 * x + 128]


def factor(basis, gathered, high, low, cells):
    f, z, columns = high.shape
    k = basis.shape[0]
    vmem = pl.BlockSpec(memory_space=pltpu.VMEM)
    return pl.pallas_call(
        factor_kernel,
        name="factor",
        out_shape=jax.ShapeDtypeStruct((f, cells, k, columns // cells), F32),
        in_specs=[vmem] * 4,
        out_specs=vmem,
        scratch_shapes=[pltpu.VMEM((k, z), F32), pltpu.VMEM((z, z), F32)] + [pltpu.VMEM((z, z), BF16)] * 3,
        compiler_params=pltpu.CompilerParams(vmem_limit_bytes=24 * 2**20),
    )(basis, gathered, high, low)


def local(velocity, initial_basis):
    n_ta, n_af = lax.axis_size("ta"), lax.axis_size("af")
    gram, high, low = regroup(velocity, n_ta, n_af)
    return factor(initial_basis.T, gram, high, low, velocity.shape[2] // n_af)


def solution(mesh):
    placed = (P(None, ("ta", "af"), None, None), P())
    return jax.shard_map(
        local, mesh=mesh, in_specs=placed, out_specs=P("ta", "af", None, None), check_vma=False
    )
```

```python
import functools
import itertools
import math
import random

import jax
import jax.numpy as jnp
from jax import lax
from jax.experimental import pallas as pl
from jax.experimental.pallas import tpu as pltpu
from jax.sharding import PartitionSpec as P

ITERS = 3
MESH = pl.DeviceIdType.MESH
HIGHEST = lax.Precision.HIGHEST
F32, BF16 = jnp.float32, jnp.bfloat16
NN = (((1,), (0,)), ((), ()))
NT = (((1,), (1,)), ((), ()))


def offsets(n_z, n_x, n_y):
    order = [o for o in itertools.product(range(n_z), range(2), range(n_x), range(n_y)) if any(o)]
    random.Random(5).shuffle(order)
    return sorted(order, key=lambda o: -hops(o, n_z, n_x, n_y))


def hops(offset, n_z, n_x, n_y):
    return sum(min(d, n - d) for d, n in ((offset[0], n_z), (offset[2], n_x), (offset[3], n_y)))


def split(value):
    high = value.astype(BF16)
    return high, (value - high.astype(F32)).astype(BF16)


def dot(a, b, dims):
    return lax.dot_general(a, b, dims, preferred_element_type=F32)


def exact(a, b, dims):
    return lax.dot_general(a, b, dims, precision=HIGHEST, preferred_element_type=F32)


def wait_bytes(ref, sem):
    pltpu.make_async_copy(ref, ref, sem).wait()


HALVES = (((0, 0), (0, 1), (1, 1), (0, 2), (0, 3)), ((1, 2), (1, 3), (2, 2), (2, 3), (3, 3)))
PAD = 16
CHUNKS = ((0, 0, 8), (1, 0, 4), (1, 4, 2), (1, 6, 2))


def regroup_kernel(
    n_ta, n_af, velocity, gathered, high, low, fibres, partial, other, packed, pieces,
    send_sem, recv_sem, own_sem, pair_send, pair_recv, rs_send, rs_recv, ag_send, ag_recv, last_send, last_recv,
):
    n = n_ta * n_af
    ta, af = lax.axis_index("ta"), lax.axis_index("af")
    me = ta * n_af + af
    core, chip = lax.rem(ta, 2), (ta // 2) * n_af + af
    partner = (ta + 1 - 2 * core, af)
    frames, planes, cells = fibres.shape[0], velocity.shape[1], fibres.shape[2]
    n_z, side = n_ta // 2, math.isqrt(n_af)
    z, x_, y_ = ta // 2, af // side, lax.rem(af, side)
    zs = [lax.rem(z + d, n_z) for d in range(n_z)]
    tas = [[2 * zs[d] + core, 2 * zs[d] + 1 - core] for d in range(n_z)]
    xs = [side * lax.rem(x_ + d, side) for d in range(side)]
    ys = [lax.rem(y_ + d, side) for d in range(side)]
    afs = [[xs[i] + ys[j] for j in range(side)] for i in range(side)]
    order = [(tas[d][c], afs[i][j]) for d, c, i, j in offsets(n_z, side, side)]
    same_core = [
        ((tas[d][0], afs[i][j]), int(hops((d, 0, i, j), n_z, side, side) > (n_z + 2 * side) // 4))
        for d, c, i, j in offsets(n_z, side, side)
        if c == 0
    ]

    def source(t, a, f, x, w):
        return velocity.at[frames * t + f, :, pl.ds(pl.multiple_of(cells * a + x, 2), w), :]

    def arrived(f, x, w):
        return fibres.at[f, pl.ds(planes * me, planes), pl.ds(x, w)]

    own = []
    for c, (f, x, w) in enumerate(CHUNKS):
        copy = pltpu.make_async_copy(source(ta, af, f, x, w), arrived(f, x, w), own_sem.at[c])
        copy.start()
        own.append(copy)

    barrier = pltpu.get_barrier_semaphore()
    for device in order:
        pl.semaphore_signal(barrier, inc=1, device_id=device, device_id_type=MESH)
    pl.semaphore_wait(barrier, n - 1)

    def send(src, dst, sems, device):
        copy = pltpu.make_async_remote_copy(
            src_ref=src, dst_ref=dst, send_sem=sems[0], recv_sem=sems[1], device_id=device, device_id_type=MESH
        )
        copy.start()
        return copy

    for c, (f, x, w) in enumerate(CHUNKS):
        for t, a in order:
            send(source(t, a, f, x, w), arrived(f, x, w), (send_sem.at[c], recv_sem.at[c]), (t, a))

    flat = fibres.reshape(frames, planes * n * cells, 128)

    def others(f, x, w):
        return fibres.at[f, pl.ds(0, planes * (n - 1)), pl.ds(x, w)]

    for c, (f, x, w) in enumerate(CHUNKS):
        own[c].wait()
        wait_bytes(others(f, x, w), recv_sem.at[c])
        for cell in range(x, x + w):
            h, l = split(flat[f, pl.ds(cell, planes * n, stride=cells), :])
            high[f, :, 128 * cell : 128 * cell + 128] = h
            low[f, :, 128 * cell : 128 * cell + 128] = l
        lanes = slice(128 * x, 128 * x + 128 * w)
        for top, left in ((0, 0), (0, 2), (2, 2)):
            rows, columns = slice(128 * top, 128 * top + 256), slice(128 * left, 128 * left + 256)
            term = (
                dot(high[f, rows, lanes], high[f, columns, lanes], NT)
                + dot(low[f, rows, lanes], high[f, columns, lanes], NT)
                + dot(high[f, rows, lanes], low[f, columns, lanes], NT)
            )
            for s, half in enumerate(HALVES):
                for k, (row, column) in enumerate(half):
                    if row - top in (0, 1) and column - left in (0, 1):
                        u, v = 128 * (row - top), 128 * (column - left)
                        block = term[u : u + 128, v : v + 128]
                        partial[s, k] = block if c == 0 else partial[s, k] + block
    for c, (f, x, w) in enumerate(CHUNKS):
        wait_bytes(others(f, x, w), send_sem.at[c])

    used = pl.ds(0, 2 * len(HALVES[0]))
    exchange = send(partial.at[1 - core], other, (pair_send, pair_recv), partner)
    exchange.wait_recv()
    flat_packed = packed.reshape(n // 2 * PAD, 128)
    for k in range(len(HALVES[0])):
        block = partial[core, k] + other[k]
        for part in range(2):
            flat_packed[pl.ds(2 * k + part, n // 2, stride=PAD), :] = block[64 * part : 64 * part + 64]
    for (t, a), _ in same_core:
        send(packed.at[(t // 2) * n_af + a, used], pieces.at[chip, used], (rs_send, rs_recv), (t, a))
    pieces[chip] = packed[chip]
    rest = pieces.at[pl.ds(0, n // 2 - 1), used]
    wait_bytes(rest, rs_recv)
    gathered[core, chip, used] = jnp.sum(pieces[:, used, :], axis=0)
    mine = gathered.at[core, chip, used]
    for device, far in same_core:
        send(mine, mine, (ag_send, ag_recv.at[far]), device)
    exchange.wait_send()
    wait_bytes(rest, rs_send)
    send(mine, mine, (last_send, last_recv), partner)
    for far in range(2):
        group = [device for device, f in same_core if f == far]
        wait_bytes(pieces.at[pl.ds(0, len(group)), used], ag_recv.at[far])
        for t, a in group:
            share = gathered.at[core, (t // 2) * n_af + a, used]
            send(share, share, (last_send, last_recv), partner)
    wait_bytes(rest, ag_send)
    wait_bytes(pieces.at[:, used], last_send)
    wait_bytes(pieces.at[:, used], last_recv)


def regroup(velocity, n_ta, n_af):
    frames, planes, cells, cells_y = velocity.shape
    n = n_ta * n_af
    f, z, x = frames // n_ta, planes * n, cells // n_af
    blocks = len(HALVES[0])
    vmem = pl.BlockSpec(memory_space=pltpu.VMEM)
    dma = pltpu.SemaphoreType.DMA
    return pl.pallas_call(
        functools.partial(regroup_kernel, n_ta, n_af),
        name="regroup",
        out_shape=(
            jax.ShapeDtypeStruct((2, n // 2, PAD, 128), F32),
            jax.ShapeDtypeStruct((f, z, x * cells_y), BF16),
            jax.ShapeDtypeStruct((f, z, x * cells_y), BF16),
        ),
        in_specs=[pl.BlockSpec(memory_space=pl.ANY)],
        out_specs=(vmem, vmem, vmem),
        scratch_shapes=[
            pltpu.VMEM((f, z, x, cells_y), F32),
            pltpu.VMEM((2, blocks, 128, 128), F32),
            pltpu.VMEM((blocks, 128, 128), F32),
            pltpu.VMEM((n // 2, PAD, 128), F32),
            pltpu.VMEM((n // 2, PAD, 128), F32),
            dma((len(CHUNKS),)), dma((len(CHUNKS),)), dma((len(CHUNKS),)),
            dma, dma, dma, dma, dma, dma((2,)), dma, dma,
        ],
        compiler_params=pltpu.CompilerParams(
            collective_id=0, has_side_effects=True, vmem_limit_bytes=48 * 2**20
        ),
    )(velocity)


def inverse_cholesky(matrix, beside):
    k, width = matrix.shape
    groups = k // 8
    rows = [matrix[8 * r : 8 * r + 8, :] for r in range(groups)]
    sublane = lax.broadcasted_iota(jnp.int32, (8, width), 0)
    spread = lambda v, c: jnp.broadcast_to(v[c : c + 1, :], (8, width))
    lane = lambda v, c: jnp.take_along_axis(v, jnp.full((8, width), c, jnp.int32), axis=1)
    pivots = []
    ahead = {}
    for g in range(groups):
        columns = [{r: ahead[d, r] if (d, r) in ahead else lane(rows[r], 8 * g + d) for r in range(g, groups)} for d in range(8)]
        late = range(g + 1, min(g + 1 + 1, groups))
        ahead = {(d, r): lane(rows[r], 8 * g + 8 + d) for r in late for d in range(8)}
        diagonal = None
        for c in range(8):
            pivot = spread(columns[c][g], c)
            diagonal = pivot if c == 0 else jnp.where(sublane == c, pivot, diagonal)
            inverse = 1.0 / pivot
            pivot_row = spread(rows[g], c)
            inside = {d: spread(columns[d][g], c) for d in range(c + 1, 8)}
            outside = {d: spread(columns[c][g + 1], d) for d in range(8)} if g + 1 < groups else {}
            for r in range(g, groups):
                factor = columns[c][r] * inverse
                if r == g:
                    factor = jnp.where(sublane > c, factor, 0.0)
                for d in range(c + 1, 8):
                    columns[d][r] = columns[d][r] - factor * inside[d]
                if r in late:
                    for d in range(8):
                        ahead[d, r] = ahead[d, r] - factor * outside[d]
                rows[r] = rows[r] - factor * pivot_row
        pivots.append(diagonal)
        if g in beside:
            beside[g]()
    scaled = []
    for r in range(groups):
        root = lax.rsqrt(pivots[r])
        root = root * (1.5 - 0.5 * (pivots[r] * root) * root)
        scaled.append(rows[r] * root)
    return jnp.concatenate(scaled, axis=0)


def factor_kernel(basis, gathered, high, low, core, subspace, gram, g1, g2, g3):
    flat = gathered.reshape(2, gathered.shape[1] * PAD, 128)
    for half, blocks in enumerate(HALVES):
        for k, (row, column) in enumerate(blocks):
            block = jnp.concatenate([flat[half, pl.ds(2 * k + p, 64, stride=PAD), :] for p in range(2)], axis=0)
            rows, columns = slice(128 * row, 128 * row + 128), slice(128 * column, 128 * column + 128)
            gram[rows, columns] = block
            if row != column:
                gram[columns, rows] = block.T
    k, z = basis.shape
    subspace[...] = basis[...]
    h, l = split(gram[...])
    g1[...] = h
    g2[...] = l
    g3[...] = (gram[...] - h.astype(F32) - l.astype(F32)).astype(BF16)
    row = lax.broadcasted_iota(jnp.int32, (k, 2 * k), 0)
    lane = lax.broadcasted_iota(jnp.int32, (k, 2 * k), 1)
    identity = jnp.where(lane == row + k, 1.0, 0.0).astype(F32)

    def times_gram(value, lanes):
        s1, s2 = split(value)
        s3 = (value - s1.astype(F32) - s2.astype(F32)).astype(BF16)
        t1 = dot(jnp.concatenate([s1, s2, s3], axis=0), g1[:, lanes], NN)
        t2 = dot(jnp.concatenate([s1, s2], axis=0), g2[:, lanes], NN)
        small = t2[k:] + (t1[2 * k :] + dot(s1, g3[:, lanes], NN))
        return small + (t1[k : 2 * k] + t2[:k]) + t1[:k]

    product = times_gram(subspace[...], slice(0, z))
    for step in range(ITERS):
        zeros = jnp.zeros_like(product)
        square = exact(product, jnp.concatenate([product, zeros], axis=0), NT)
        beside = {}
        if step < ITERS - 1:

            def piece(i, value=product):
                lanes = slice(i * z // 1, (i + 1) * z // 1)
                subspace[:, lanes] = times_gram(value, lanes)

            beside = {g: functools.partial(piece, i) for i, g in enumerate((0,))}
        inverse = inverse_cholesky(square + identity, beside)
        target = subspace[...] if step < ITERS - 1 else product
        product = exact(inverse, jnp.concatenate([zeros, target], axis=0), NN)
    subspace[...] = product
    s_high, s_low = split(subspace[...])
    both = jnp.concatenate([s_high, s_low], axis=0)
    for f in range(high.shape[0]):
        first = dot(both, high[f], NN)
        result = first[:k] + first[k:] + dot(s_high, low[f], NN)
        for x in range(core.shape[1]):
            core[f, x] = result[:, 128 * x : 128 * x + 128]


def factor(basis, gathered, high, low, cells):
    f, z, columns = high.shape
    k = basis.shape[0]
    vmem = pl.BlockSpec(memory_space=pltpu.VMEM)
    return pl.pallas_call(
        factor_kernel,
        name="factor",
        out_shape=jax.ShapeDtypeStruct((f, cells, k, columns // cells), F32),
        in_specs=[vmem] * 4,
        out_specs=vmem,
        scratch_shapes=[pltpu.VMEM((k, z), F32), pltpu.VMEM((z, z), F32)] + [pltpu.VMEM((z, z), BF16)] * 3,
        compiler_params=pltpu.CompilerParams(vmem_limit_bytes=24 * 2**20),
    )(basis, gathered, high, low)


def local(velocity, initial_basis):
    n_ta, n_af = lax.axis_size("ta"), lax.axis_size("af")
    gram, high, low = regroup(velocity, n_ta, n_af)
    return factor(initial_basis.T, gram, high, low, velocity.shape[2] // n_af)


def solution(mesh):
    placed = (P(None, ("ta", "af"), None, None), P())
    return jax.shard_map(
        local, mesh=mesh, in_specs=placed, out_specs=P("ta", "af", None, None), check_vma=False
    )
```

```python
import functools
import itertools
import math
import random

import jax
import jax.numpy as jnp
from jax import lax
from jax.experimental import pallas as pl
from jax.experimental.pallas import tpu as pltpu
from jax.sharding import PartitionSpec as P

ITERS = 3
MESH = pl.DeviceIdType.MESH
HIGHEST = lax.Precision.HIGHEST
F32, BF16 = jnp.float32, jnp.bfloat16
NN = (((1,), (0,)), ((), ()))
NT = (((1,), (1,)), ((), ()))


def offsets(n_z, n_x, n_y):
    order = [o for o in itertools.product(range(n_z), range(2), range(n_x), range(n_y)) if any(o)]
    random.Random(5).shuffle(order)
    return sorted(order, key=lambda o: -hops(o, n_z, n_x, n_y))


def hops(offset, n_z, n_x, n_y):
    return sum(min(d, n - d) for d, n in ((offset[0], n_z), (offset[2], n_x), (offset[3], n_y)))


def split(value):
    high = value.astype(BF16)
    return high, (value - high.astype(F32)).astype(BF16)


def dot(a, b, dims):
    return lax.dot_general(a, b, dims, preferred_element_type=F32)


def exact(a, b, dims):
    return lax.dot_general(a, b, dims, precision=HIGHEST, preferred_element_type=F32)


def wait_bytes(ref, sem):
    pltpu.make_async_copy(ref, ref, sem).wait()


HALVES = (((0, 0), (0, 1), (1, 1), (0, 2), (0, 3)), ((1, 2), (1, 3), (2, 2), (2, 3), (3, 3)))
PAD = 16
CHUNKS = ((0, 0, 8), (1, 0, 4), (1, 4, 2), (1, 6, 2))


def regroup_kernel(
    n_ta, n_af, velocity, gathered, high, low, fibres, partial, other, packed, pieces,
    send_sem, recv_sem, own_sem, pair_send, pair_recv, rs_send, rs_recv, ag_send, ag_recv, last_send, last_recv,
):
    n = n_ta * n_af
    ta, af = lax.axis_index("ta"), lax.axis_index("af")
    me = ta * n_af + af
    core, chip = lax.rem(ta, 2), (ta // 2) * n_af + af
    partner = (ta + 1 - 2 * core, af)
    frames, planes, cells = fibres.shape[0], velocity.shape[1], fibres.shape[2]
    n_z, side = n_ta // 2, math.isqrt(n_af)
    z, x_, y_ = ta // 2, af // side, lax.rem(af, side)
    zs = [lax.rem(z + d, n_z) for d in range(n_z)]
    tas = [[2 * zs[d] + core, 2 * zs[d] + 1 - core] for d in range(n_z)]
    xs = [side * lax.rem(x_ + d, side) for d in range(side)]
    ys = [lax.rem(y_ + d, side) for d in range(side)]
    afs = [[xs[i] + ys[j] for j in range(side)] for i in range(side)]
    order = [(tas[d][c], afs[i][j]) for d, c, i, j in offsets(n_z, side, side)]
    same_core = [
        ((tas[d][0], afs[i][j]), int(hops((d, 0, i, j), n_z, side, side) > (n_z + 2 * side) // 4))
        for d, c, i, j in offsets(n_z, side, side)
        if c == 0
    ]

    def source(t, a, f, x, w):
        return velocity.at[frames * t + f, :, pl.ds(pl.multiple_of(cells * a + x, 2), w), :]

    def arrived(f, x, w):
        return fibres.at[f, pl.ds(planes * me, planes), pl.ds(x, w)]

    own = []
    for c, (f, x, w) in enumerate(CHUNKS):
        copy = pltpu.make_async_copy(source(ta, af, f, x, w), arrived(f, x, w), own_sem.at[c])
        copy.start()
        own.append(copy)

    barrier = pltpu.get_barrier_semaphore()
    for device in order:
        pl.semaphore_signal(barrier, inc=1, device_id=device, device_id_type=MESH)
    pl.semaphore_wait(barrier, n - 1)

    def send(src, dst, sems, device):
        copy = pltpu.make_async_remote_copy(
            src_ref=src, dst_ref=dst, send_sem=sems[0], recv_sem=sems[1], device_id=device, device_id_type=MESH
        )
        copy.start()
        return copy

    for c, (f, x, w) in enumerate(CHUNKS):
        for t, a in order:
            send(source(t, a, f, x, w), arrived(f, x, w), (send_sem.at[c], recv_sem.at[c]), (t, a))

    flat = fibres.reshape(frames, planes * n * cells, 128)

    def others(f, x, w):
        return fibres.at[f, pl.ds(0, planes * (n - 1)), pl.ds(x, w)]

    for c, (f, x, w) in enumerate(CHUNKS):
        own[c].wait()
        wait_bytes(others(f, x, w), recv_sem.at[c])
        for cell in range(x, x + w):
            h, l = split(flat[f, pl.ds(cell, planes * n, stride=cells), :])
            high[f, :, 128 * cell : 128 * cell + 128] = h
            low[f, :, 128 * cell : 128 * cell + 128] = l
        lanes = slice(128 * x, 128 * x + 128 * w)
        for top, left in ((0, 0), (0, 2), (2, 2)):
            rows, columns = slice(128 * top, 128 * top + 256), slice(128 * left, 128 * left + 256)
            term = (
                dot(high[f, rows, lanes], high[f, columns, lanes], NT)
                + dot(low[f, rows, lanes], high[f, columns, lanes], NT)
                + dot(high[f, rows, lanes], low[f, columns, lanes], NT)
            )
            for s, half in enumerate(HALVES):
                for k, (row, column) in enumerate(half):
                    if row - top in (0, 1) and column - left in (0, 1):
                        u, v = 128 * (row - top), 128 * (column - left)
                        block = term[u : u + 128, v : v + 128]
                        partial[s, k] = block if c == 0 else partial[s, k] + block
    for c, (f, x, w) in enumerate(CHUNKS):
        wait_bytes(others(f, x, w), send_sem.at[c])

    used = pl.ds(0, 2 * len(HALVES[0]))
    exchange = send(partial.at[1 - core], other, (pair_send, pair_recv), partner)
    exchange.wait_recv()
    flat_packed = packed.reshape(n // 2 * PAD, 128)
    for k in range(len(HALVES[0])):
        block = partial[core, k] + other[k]
        for part in range(2):
            flat_packed[pl.ds(2 * k + part, n // 2, stride=PAD), :] = block[64 * part : 64 * part + 64]
    for (t, a), _ in same_core:
        send(packed.at[(t // 2) * n_af + a, used], pieces.at[chip, used], (rs_send, rs_recv), (t, a))
    pieces[chip] = packed[chip]
    rest = pieces.at[pl.ds(0, n // 2 - 1), used]
    wait_bytes(rest, rs_recv)
    gathered[core, chip, used] = jnp.sum(pieces[:, used, :], axis=0)
    mine = gathered.at[core, chip, used]
    for device, far in same_core:
        send(mine, mine, (ag_send, ag_recv.at[far]), device)
    exchange.wait_send()
    wait_bytes(rest, rs_send)
    send(mine, mine, (last_send, last_recv), partner)
    for far in range(2):
        group = [device for device, f in same_core if f == far]
        wait_bytes(pieces.at[pl.ds(0, len(group)), used], ag_recv.at[far])
        for t, a in group:
            share = gathered.at[core, (t // 2) * n_af + a, used]
            send(share, share, (last_send, last_recv), partner)
    wait_bytes(rest, ag_send)
    wait_bytes(pieces.at[:, used], last_send)
    wait_bytes(pieces.at[:, used], last_recv)


def regroup(velocity, n_ta, n_af):
    frames, planes, cells, cells_y = velocity.shape
    n = n_ta * n_af
    f, z, x = frames // n_ta, planes * n, cells // n_af
    blocks = len(HALVES[0])
    vmem = pl.BlockSpec(memory_space=pltpu.VMEM)
    dma = pltpu.SemaphoreType.DMA
    return pl.pallas_call(
        functools.partial(regroup_kernel, n_ta, n_af),
        name="regroup",
        out_shape=(
            jax.ShapeDtypeStruct((2, n // 2, PAD, 128), F32),
            jax.ShapeDtypeStruct((f, z, x * cells_y), BF16),
            jax.ShapeDtypeStruct((f, z, x * cells_y), BF16),
        ),
        in_specs=[pl.BlockSpec(memory_space=pl.ANY)],
        out_specs=(vmem, vmem, vmem),
        scratch_shapes=[
            pltpu.VMEM((f, z, x, cells_y), F32),
            pltpu.VMEM((2, blocks, 128, 128), F32),
            pltpu.VMEM((blocks, 128, 128), F32),
            pltpu.VMEM((n // 2, PAD, 128), F32),
            pltpu.VMEM((n // 2, PAD, 128), F32),
            dma((len(CHUNKS),)), dma((len(CHUNKS),)), dma((len(CHUNKS),)),
            dma, dma, dma, dma, dma, dma((2,)), dma, dma,
        ],
        compiler_params=pltpu.CompilerParams(
            collective_id=0, has_side_effects=True, vmem_limit_bytes=48 * 2**20
        ),
    )(velocity)


def inverse_cholesky(matrix, beside):
    k, width = matrix.shape
    groups = k // 8
    rows = [matrix[8 * r : 8 * r + 8, :] for r in range(groups)]
    sublane = lax.broadcasted_iota(jnp.int32, (8, width), 0)
    spread = lambda v, c: jnp.broadcast_to(v[c : c + 1, :], (8, width))
    lane = lambda v, c: jnp.take_along_axis(v, jnp.full((8, width), c, jnp.int32), axis=1)
    pivots = []
    ahead = {}
    pivot = spread(lane(rows[0], 0), 0)
    for g in range(groups):
        columns = [{r: ahead[d, r] if (d, r) in ahead else lane(rows[r], 8 * g + d) for r in range(g, groups)} for d in range(8)]
        late = range(g + 1, min(g + 1 + 1, groups))
        ahead = {(d, r): lane(rows[r], 8 * g + 8 + d) for r in late for d in range(8)}
        diagonal = None
        for c in range(8):
            diagonal = pivot if c == 0 else jnp.where(sublane == c, pivot, diagonal)
            inverse = 1.0 / pivot
            pivot_row = spread(rows[g], c)
            inside = {d: spread(columns[d][g], c) for d in range(c + 1, 8)}
            outside = {d: spread(columns[c][g + 1], d) for d in range(8)} if g + 1 < groups else {}
            if c < 7:
                pivot = spread(columns[c + 1][g], c + 1) - (spread(columns[c][g], c + 1) * inverse) * inside[c + 1]
            elif g + 1 < groups:
                pivot = spread(ahead[0, g + 1], 0) - (outside[0] * inverse) * outside[0]
            for r in range(g, groups):
                factor = columns[c][r] * inverse
                if r == g:
                    factor = jnp.where(sublane > c, factor, 0.0)
                for d in range(c + 1, 8):
                    columns[d][r] = columns[d][r] - factor * inside[d]
                if r in late:
                    for d in range(8):
                        ahead[d, r] = ahead[d, r] - factor * outside[d]
                rows[r] = rows[r] - factor * pivot_row
        pivots.append(diagonal)
        if g in beside:
            beside[g]()
    scaled = []
    for r in range(groups):
        root = lax.rsqrt(pivots[r])
        root = root * (1.5 - 0.5 * (pivots[r] * root) * root)
        scaled.append(rows[r] * root)
    return jnp.concatenate(scaled, axis=0)


def factor_kernel(basis, gathered, high, low, core, subspace, gram, g1, g2, g3, staged, sem):
    flat = gathered.reshape(2, gathered.shape[1] * PAD, 128)
    for half, blocks in enumerate(HALVES):
        for k, (row, column) in enumerate(blocks):
            block = jnp.concatenate([flat[half, pl.ds(2 * k + p, 64, stride=PAD), :] for p in range(2)], axis=0)
            rows, columns = slice(128 * row, 128 * row + 128), slice(128 * column, 128 * column + 128)
            gram[rows, columns] = block
            if row != column:
                gram[columns, rows] = block.T
    k, z = basis.shape
    subspace[...] = basis[...]
    h, l = split(gram[...])
    g1[...] = h
    g2[...] = l
    g3[...] = (gram[...] - h.astype(F32) - l.astype(F32)).astype(BF16)
    row = lax.broadcasted_iota(jnp.int32, (k, 2 * k), 0)
    lane = lax.broadcasted_iota(jnp.int32, (k, 2 * k), 1)
    identity = jnp.where(lane == row + k, 1.0, 0.0).astype(F32)

    def times_gram(value, lanes):
        s1, s2 = split(value)
        s3 = (value - s1.astype(F32) - s2.astype(F32)).astype(BF16)
        t1 = dot(jnp.concatenate([s1, s2, s3], axis=0), g1[:, lanes], NN)
        t2 = dot(jnp.concatenate([s1, s2], axis=0), g2[:, lanes], NN)
        small = t2[k:] + (t1[2 * k :] + dot(s1, g3[:, lanes], NN))
        return small + (t1[k : 2 * k] + t2[:k]) + t1[:k]

    product = times_gram(subspace[...], slice(0, z))
    for step in range(ITERS):
        zeros = jnp.zeros_like(product)
        square = exact(product, jnp.concatenate([product, zeros], axis=0), NT)
        beside = {}
        if step < ITERS - 1:

            def piece(i, value=product):
                lanes = slice(i * z // 1, (i + 1) * z // 1)
                subspace[:, lanes] = times_gram(value, lanes)

            beside = {g: functools.partial(piece, i) for i, g in enumerate((0,))}
        inverse = inverse_cholesky(square + identity, beside)
        target = subspace[...] if step < ITERS - 1 else product
        product = exact(inverse, jnp.concatenate([zeros, target], axis=0), NN)
    subspace[...] = product
    s_high, s_low = split(subspace[...])
    both = jnp.concatenate([s_high, s_low], axis=0)
    copies = []
    for f in range(high.shape[0]):
        first = dot(both, high[f], NN)
        result = first[:k] + first[k:] + dot(s_high, low[f], NN)
        for x in range(staged.shape[1]):
            staged[f, x] = result[:, 128 * x : 128 * x + 128]
        copy = pltpu.make_async_copy(staged.at[f], core.at[f], sem.at[f])
        copy.start()
        copies.append(copy)
    for copy in copies:
        copy.wait()


def factor(basis, gathered, high, low, cells):
    f, z, columns = high.shape
    k = basis.shape[0]
    vmem = pl.BlockSpec(memory_space=pltpu.VMEM)
    return pl.pallas_call(
        factor_kernel,
        name="factor",
        out_shape=jax.ShapeDtypeStruct((f, cells, k, columns // cells), F32),
        in_specs=[vmem] * 4,
        out_specs=pl.BlockSpec(memory_space=pl.ANY),
        scratch_shapes=[pltpu.VMEM((k, z), F32), pltpu.VMEM((z, z), F32)]
        + [pltpu.VMEM((z, z), BF16)] * 3
        + [pltpu.VMEM((f, cells, k, columns // cells), F32), pltpu.SemaphoreType.DMA((f,))],
        compiler_params=pltpu.CompilerParams(vmem_limit_bytes=24 * 2**20),
    )(basis, gathered, high, low)


def local(velocity, initial_basis):
    n_ta, n_af = lax.axis_size("ta"), lax.axis_size("af")
    gram, high, low = regroup(velocity, n_ta, n_af)
    return factor(initial_basis.T, gram, high, low, velocity.shape[2] // n_af)


def solution(mesh):
    placed = (P(None, ("ta", "af"), None, None), P())
    return jax.shard_map(
        local, mesh=mesh, in_specs=placed, out_specs=P("ta", "af", None, None), check_vma=False
    )
```

```python
import functools
import itertools
import math
import random

import jax
import jax.numpy as jnp
from jax import lax
from jax.experimental import pallas as pl
from jax.experimental.pallas import tpu as pltpu
from jax.sharding import PartitionSpec as P

ITERS = 3
MESH = pl.DeviceIdType.MESH
HIGHEST = lax.Precision.HIGHEST
F32, BF16 = jnp.float32, jnp.bfloat16
NN = (((1,), (0,)), ((), ()))
NT = (((1,), (1,)), ((), ()))


def offsets(n_z, n_x, n_y):
    order = [o for o in itertools.product(range(n_z), range(2), range(n_x), range(n_y)) if any(o)]
    random.Random(5).shuffle(order)
    return sorted(order, key=lambda o: -hops(o, n_z, n_x, n_y))


def hops(offset, n_z, n_x, n_y):
    return sum(min(d, n - d) for d, n in ((offset[0], n_z), (offset[2], n_x), (offset[3], n_y)))


def split(value):
    high = value.astype(BF16)
    return high, (value - high.astype(F32)).astype(BF16)


def dot(a, b, dims):
    return lax.dot_general(a, b, dims, preferred_element_type=F32)


def exact(a, b, dims):
    return lax.dot_general(a, b, dims, precision=HIGHEST, preferred_element_type=F32)


def wait_bytes(ref, sem):
    pltpu.make_async_copy(ref, ref, sem).wait()


HALVES = (((0, 0), (0, 1), (1, 1), (0, 2), (0, 3)), ((1, 2), (1, 3), (2, 2), (2, 3), (3, 3)))
PAD = 16
CHUNKS = ((0, 0, 8), (1, 0, 4), (1, 4, 4))


def regroup_kernel(
    n_ta, n_af, velocity, gathered, high, low, fibres, partial, other, packed, pieces,
    send_sem, recv_sem, own_sem, pair_send, pair_recv, rs_send, rs_recv, ag_send, ag_recv, last_send, last_recv,
):
    n = n_ta * n_af
    ta, af = lax.axis_index("ta"), lax.axis_index("af")
    me = ta * n_af + af
    core, chip = lax.rem(ta, 2), (ta // 2) * n_af + af
    partner = (ta + 1 - 2 * core, af)
    frames, planes, cells = fibres.shape[0], velocity.shape[1], fibres.shape[2]
    n_z, side = n_ta // 2, math.isqrt(n_af)
    z, x_, y_ = ta // 2, af // side, lax.rem(af, side)
    zs = [lax.rem(z + d, n_z) for d in range(n_z)]
    tas = [[2 * zs[d] + core, 2 * zs[d] + 1 - core] for d in range(n_z)]
    xs = [side * lax.rem(x_ + d, side) for d in range(side)]
    ys = [lax.rem(y_ + d, side) for d in range(side)]
    afs = [[xs[i] + ys[j] for j in range(side)] for i in range(side)]
    order = [(tas[d][c], afs[i][j]) for d, c, i, j in offsets(n_z, side, side)]
    same_core = [
        ((tas[d][0], afs[i][j]), int(hops((d, 0, i, j), n_z, side, side) > (n_z + 2 * side) // 4))
        for d, c, i, j in offsets(n_z, side, side)
        if c == 0
    ]

    def source(t, a, f, x, w):
        return velocity.at[frames * t + f, :, pl.ds(pl.multiple_of(cells * a + x, 2), w), :]

    def arrived(f, x, w):
        return fibres.at[f, pl.ds(planes * me, planes), pl.ds(x, w)]

    own = []
    for c, (f, x, w) in enumerate(CHUNKS):
        copy = pltpu.make_async_copy(source(ta, af, f, x, w), arrived(f, x, w), own_sem.at[c])
        copy.start()
        own.append(copy)

    barrier = pltpu.get_barrier_semaphore()
    for device in order:
        pl.semaphore_signal(barrier, inc=1, device_id=device, device_id_type=MESH)
    pl.semaphore_wait(barrier, n - 1)

    def send(src, dst, sems, device):
        copy = pltpu.make_async_remote_copy(
            src_ref=src, dst_ref=dst, send_sem=sems[0], recv_sem=sems[1], device_id=device, device_id_type=MESH
        )
        copy.start()
        return copy

    for c, (f, x, w) in enumerate(CHUNKS):
        for t, a in order:
            send(source(t, a, f, x, w), arrived(f, x, w), (send_sem.at[c], recv_sem.at[c]), (t, a))

    flat = fibres.reshape(frames, planes * n * cells, 128)

    def others(f, x, w):
        return fibres.at[f, pl.ds(0, planes * (n - 1)), pl.ds(x, w)]

    for c, (f, x, w) in enumerate(CHUNKS):
        own[c].wait()
        wait_bytes(others(f, x, w), recv_sem.at[c])
        for cell in range(x, x + w):
            h, l = split(flat[f, pl.ds(cell, planes * n, stride=cells), :])
            high[f, :, 128 * cell : 128 * cell + 128] = h
            low[f, :, 128 * cell : 128 * cell + 128] = l
        lanes = slice(128 * x, 128 * x + 128 * w)
        for top, left in ((0, 0), (0, 2), (2, 2)):
            rows, columns = slice(128 * top, 128 * top + 256), slice(128 * left, 128 * left + 256)
            term = (
                dot(high[f, rows, lanes], high[f, columns, lanes], NT)
                + dot(low[f, rows, lanes], high[f, columns, lanes], NT)
                + dot(high[f, rows, lanes], low[f, columns, lanes], NT)
            )
            for s, half in enumerate(HALVES):
                for k, (row, column) in enumerate(half):
                    if row - top in (0, 1) and column - left in (0, 1):
                        u, v = 128 * (row - top), 128 * (column - left)
                        block = term[u : u + 128, v : v + 128]
                        partial[s, k] = block if c == 0 else partial[s, k] + block
    for c, (f, x, w) in enumerate(CHUNKS):
        wait_bytes(others(f, x, w), send_sem.at[c])

    used = pl.ds(0, 2 * len(HALVES[0]))
    exchange = send(partial.at[1 - core], other, (pair_send, pair_recv), partner)
    exchange.wait_recv()
    flat_packed = packed.reshape(n // 2 * PAD, 128)
    for k in range(len(HALVES[0])):
        block = partial[core, k] + other[k]
        for part in range(2):
            flat_packed[pl.ds(2 * k + part, n // 2, stride=PAD), :] = block[64 * part : 64 * part + 64]
    for (t, a), _ in same_core:
        send(packed.at[(t // 2) * n_af + a, used], pieces.at[chip, used], (rs_send, rs_recv), (t, a))
    pieces[chip] = packed[chip]
    rest = pieces.at[pl.ds(0, n // 2 - 1), used]
    wait_bytes(rest, rs_recv)
    gathered[core, chip, used] = jnp.sum(pieces[:, used, :], axis=0)
    mine = gathered.at[core, chip, used]
    for device, far in same_core:
        send(mine, mine, (ag_send, ag_recv.at[far]), device)
    exchange.wait_send()
    wait_bytes(rest, rs_send)
    send(mine, mine, (last_send, last_recv), partner)
    for far in range(2):
        group = [device for device, f in same_core if f == far]
        wait_bytes(pieces.at[pl.ds(0, len(group)), used], ag_recv.at[far])
        for t, a in group:
            share = gathered.at[core, (t // 2) * n_af + a, used]
            send(share, share, (last_send, last_recv), partner)
    wait_bytes(rest, ag_send)
    wait_bytes(pieces.at[:, used], last_send)
    wait_bytes(pieces.at[:, used], last_recv)


def regroup(velocity, n_ta, n_af):
    frames, planes, cells, cells_y = velocity.shape
    n = n_ta * n_af
    f, z, x = frames // n_ta, planes * n, cells // n_af
    blocks = len(HALVES[0])
    vmem = pl.BlockSpec(memory_space=pltpu.VMEM)
    dma = pltpu.SemaphoreType.DMA
    return pl.pallas_call(
        functools.partial(regroup_kernel, n_ta, n_af),
        name="regroup",
        out_shape=(
            jax.ShapeDtypeStruct((2, n // 2, PAD, 128), F32),
            jax.ShapeDtypeStruct((f, z, x * cells_y), BF16),
            jax.ShapeDtypeStruct((f, z, x * cells_y), BF16),
        ),
        in_specs=[pl.BlockSpec(memory_space=pl.ANY)],
        out_specs=(vmem, vmem, vmem),
        scratch_shapes=[
            pltpu.VMEM((f, z, x, cells_y), F32),
            pltpu.VMEM((2, blocks, 128, 128), F32),
            pltpu.VMEM((blocks, 128, 128), F32),
            pltpu.VMEM((n // 2, PAD, 128), F32),
            pltpu.VMEM((n // 2, PAD, 128), F32),
            dma((len(CHUNKS),)), dma((len(CHUNKS),)), dma((len(CHUNKS),)),
            dma, dma, dma, dma, dma, dma((2,)), dma, dma,
        ],
        compiler_params=pltpu.CompilerParams(
            collective_id=0, has_side_effects=True, vmem_limit_bytes=48 * 2**20
        ),
    )(velocity)


def inverse_cholesky(matrix, beside):
    k, width = matrix.shape
    groups = k // 8
    rows = [matrix[8 * r : 8 * r + 8, :] for r in range(groups)]
    sublane = lax.broadcasted_iota(jnp.int32, (8, width), 0)
    spread = lambda v, c: jnp.broadcast_to(v[c : c + 1, :], (8, width))
    lane = lambda v, c: jnp.take_along_axis(v, jnp.full((8, width), c, jnp.int32), axis=1)
    pivots = []
    ahead = {}
    pivot = spread(lane(rows[0], 0), 0)
    for g in range(groups):
        columns = [{r: ahead[d, r] if (d, r) in ahead else lane(rows[r], 8 * g + d) for r in range(g, groups)} for d in range(8)]
        late = range(g + 1, min(g + 1 + 1, groups))
        ahead = {(d, r): lane(rows[r], 8 * g + 8 + d) for r in late for d in range(8)}
        diagonal = None
        for c in range(8):
            diagonal = pivot if c == 0 else jnp.where(sublane == c, pivot, diagonal)
            inverse = 1.0 / pivot
            pivot_row = spread(rows[g], c)
            inside = {d: spread(columns[d][g], c) for d in range(c + 1, 8)}
            outside = {d: spread(columns[c][g + 1], d) for d in range(8)} if g + 1 < groups else {}
            if c < 7:
                pivot = spread(columns[c + 1][g], c + 1) - (spread(columns[c][g], c + 1) * inverse) * inside[c + 1]
            elif g + 1 < groups:
                pivot = spread(ahead[0, g + 1], 0) - (outside[0] * inverse) * outside[0]
            for r in range(g, groups):
                factor = columns[c][r] * inverse
                if r == g:
                    factor = jnp.where(sublane > c, factor, 0.0)
                for d in range(c + 1, 8):
                    columns[d][r] = columns[d][r] - factor * inside[d]
                if r in late:
                    for d in range(8):
                        ahead[d, r] = ahead[d, r] - factor * outside[d]
                rows[r] = rows[r] - factor * pivot_row
        pivots.append(diagonal)
        if g in beside:
            beside[g]()
    scaled = []
    for r in range(groups):
        root = lax.rsqrt(pivots[r])
        root = root * (1.5 - 0.5 * (pivots[r] * root) * root)
        scaled.append(rows[r] * root)
    return jnp.concatenate(scaled, axis=0)


def factor_kernel(basis, gathered, high, low, core, subspace, gram, g1, g2, g3, staged, sem):
    flat = gathered.reshape(2, gathered.shape[1] * PAD, 128)
    for half, blocks in enumerate(HALVES):
        for k, (row, column) in enumerate(blocks):
            block = jnp.concatenate([flat[half, pl.ds(2 * k + p, 64, stride=PAD), :] for p in range(2)], axis=0)
            rows, columns = slice(128 * row, 128 * row + 128), slice(128 * column, 128 * column + 128)
            gram[rows, columns] = block
            if row != column:
                gram[columns, rows] = block.T
    k, z = basis.shape
    subspace[...] = basis[...]
    h, l = split(gram[...])
    g1[...] = h
    g2[...] = l
    g3[...] = (gram[...] - h.astype(F32) - l.astype(F32)).astype(BF16)
    row = lax.broadcasted_iota(jnp.int32, (k, 2 * k), 0)
    lane = lax.broadcasted_iota(jnp.int32, (k, 2 * k), 1)
    identity = jnp.where(lane == row + k, 1.0, 0.0).astype(F32)

    def times_gram(value, lanes):
        s1, s2 = split(value)
        s3 = (value - s1.astype(F32) - s2.astype(F32)).astype(BF16)
        t1 = dot(jnp.concatenate([s1, s2, s3], axis=0), g1[:, lanes], NN)
        t2 = dot(jnp.concatenate([s1, s2], axis=0), g2[:, lanes], NN)
        small = t2[k:] + (t1[2 * k :] + dot(s1, g3[:, lanes], NN))
        return small + (t1[k : 2 * k] + t2[:k]) + t1[:k]

    product = times_gram(subspace[...], slice(0, z))
    for step in range(ITERS):
        zeros = jnp.zeros_like(product)
        square = exact(product, jnp.concatenate([product, zeros], axis=0), NT)
        beside = {}
        if step < ITERS - 1:

            def piece(i, value=product):
                lanes = slice(i * z // 1, (i + 1) * z // 1)
                subspace[:, lanes] = times_gram(value, lanes)

            beside = {g: functools.partial(piece, i) for i, g in enumerate((0,))}
        inverse = inverse_cholesky(square + identity, beside)
        target = subspace[...] if step < ITERS - 1 else product
        product = exact(inverse, jnp.concatenate([zeros, target], axis=0), NN)
    subspace[...] = product
    s_high, s_low = split(subspace[...])
    both = jnp.concatenate([s_high, s_low], axis=0)
    copies = []
    for f in range(high.shape[0]):
        first = dot(both, high[f], NN)
        result = first[:k] + first[k:] + dot(s_high, low[f], NN)
        for x in range(staged.shape[1]):
            staged[f, x] = result[:, 128 * x : 128 * x + 128]
        copy = pltpu.make_async_copy(staged.at[f], core.at[f], sem.at[f])
        copy.start()
        copies.append(copy)
    for copy in copies:
        copy.wait()


def factor(basis, gathered, high, low, cells):
    f, z, columns = high.shape
    k = basis.shape[0]
    vmem = pl.BlockSpec(memory_space=pltpu.VMEM)
    return pl.pallas_call(
        factor_kernel,
        name="factor",
        out_shape=jax.ShapeDtypeStruct((f, cells, k, columns // cells), F32),
        in_specs=[vmem] * 4,
        out_specs=pl.BlockSpec(memory_space=pl.ANY),
        scratch_shapes=[pltpu.VMEM((k, z), F32), pltpu.VMEM((z, z), F32)]
        + [pltpu.VMEM((z, z), BF16)] * 3
        + [pltpu.VMEM((f, cells, k, columns // cells), F32), pltpu.SemaphoreType.DMA((f,))],
        compiler_params=pltpu.CompilerParams(vmem_limit_bytes=24 * 2**20),
    )(basis, gathered, high, low)


def local(velocity, initial_basis):
    n_ta, n_af = lax.axis_size("ta"), lax.axis_size("af")
    gram, high, low = regroup(velocity, n_ta, n_af)
    return factor(initial_basis.T, gram, high, low, velocity.shape[2] // n_af)


def solution(mesh):
    placed = (P(None, ("ta", "af"), None, None), P())
    return jax.shard_map(
        local, mesh=mesh, in_specs=placed, out_specs=P("ta", "af", None, None), check_vma=False
    )
```
